256 devices in a mesh: expert: 64 (over y, z, core), tensor: 4 (over x).
Axes of the slice: x: 4, y: 4, z: 8, core: 2. Of those that a mesh axis runs over, the one named last changes fastest.
Arguments:
- attn_heads: bfloat16 [8192, 4096], P('expert', 'tensor'), may hold values from -6 to 6
- out_proj: bfloat16 [4096, 4096], P('tensor', 'expert'), may hold values from -0.09375 to 0.09375
- residual: bfloat16 [8192, 4096], P('expert'), may hold values from -6 to 6
- norm_gain: float32 [4096], replicated, may hold values from 0.1 to 1.9
- route_ids: int32 [8192, 8], P('expert'), may hold values from 0 to 63, all different within a row; in each aligned block of 128 rows (0 to 127, 128 to 255, ...) at most 18 rows name the same one
- route_weights: float32 [8192, 8], P('expert'), may hold values from 0.05 to 1
- w_gate: bfloat16 [64, 4096, 1536], P('expert', None, 'tensor'), may hold values from -0.09375 to 0.09375
- w_up: bfloat16 [64, 4096, 1536], P('expert', None, 'tensor'), may hold values from -0.09375 to 0.09375
- w_down: bfloat16 [64, 1536, 4096], P('expert', 'tensor'), may hold values from -0.15625 to 0.15625
Outputs:
- layer_out: bfloat16 [8192, 4096], P('expert', 'tensor')
The draws below stay inside these ranges and needn't reach their ends.
Inputs may be any that keep to these rules, and one draw needn't show every extreme that they name: `route_ids`: each row names 8 different experts. In aligned blocks of 128 rows no expert is named more than 18 times, a bound that some block reaches.
All inputs are finite; a program needn't handle non-finite values.
Results may differ from the reference program's by a relative error of at most 0.015.
Values may be sent and summed in bfloat16 or wider, within the bound.
A program may use at most 128 MiB of HBM per device.

```python
import math
import jax
import jax.numpy as jnp
import numpy as np
from jax import lax

D = 4096
HEADS = 32
HD = 128
FF = 1536
EXPERTS = 64
TOP = 8
TOK_DEV = 128
CAP = 18
TOKENS = 8192
N_EXPERT = 64
N_TENSOR = 4


def block_levels(rng, dims, cuts, least, top_value):
    def one(axis_at, blocks):
        draws = jax.random.uniform(jax.random.fold_in(jax.random.fold_in(rng, 6), axis_at), (blocks,), jnp.float32, least / len(cuts), top_value / len(cuts))
        return jnp.repeat(jnp.exp(draws), dims[axis_at] // blocks).reshape((-1,) + (1,) * (len(dims) - axis_at - 1))

    factor_of = one(*cuts[0])
    for cut in cuts[1:]:
        factor_of = factor_of * one(*cut)
    return factor_of


def deal_out(stream_key, own, number, rows, count, top, reach, slope):
    sequence = jax.random.permutation(stream_key, count)
    crowded, ordinary = load_shares(count, rows * top, reach, slope, True), load_shares(count, rows * top, reach, slope, False)
    places = jnp.arange(count)

    def named(sizes, turn):
        used = int((sizes > 0).sum())
        fixed = max(1, used // 4)
        passed = fixed + (places - fixed + turn * (used - fixed)) % max(1, count - fixed)
        return jnp.zeros((count,), jnp.int32).at[sequence[jnp.where(places < fixed, places, passed)]].set(jnp.asarray(sizes, jnp.int32))

    sizes = jnp.where(number % 4 == 0, named(crowded, number // 4), named(ordinary, number - number // 4 - 1))
    mixed = jax.random.permutation(jax.random.fold_in(own, 3), count)
    donor, receiver = mixed[0:count // 2 * 2:2], mixed[1:count // 2 * 2:2]
    margin = jnp.minimum(sizes[donor] - 1, reach - sizes[receiver]) // 2
    margin = jnp.where((donor == sequence[0]) | (receiver == sequence[0]) | (sizes[receiver] == 0), 0, jnp.maximum(margin, 0))
    passed = jax.random.randint(jax.random.fold_in(own, 4), (count // 2,), 0, 1 << 20) % (margin + 1)
    sizes = sizes.at[donor].add(-passed).at[receiver].add(passed)
    labels = jnp.searchsorted(jnp.cumsum(sizes), jnp.arange(rows * top), side="right").astype(jnp.int32)
    grid = labels.reshape(top, rows).T
    grid = grid[jax.random.permutation(jax.random.fold_in(own, 1), rows)]
    turn = jax.random.randint(jax.random.fold_in(own, 2), (rows, 1), 0, top)
    return jnp.take_along_axis(grid, (jnp.arange(top)[None, :] + turn) % top, axis=1)


def load_shares(number_of, total, reach, skew, full):
    loads = [(1 << 20) // math.isqrt(rank ** skew) + 1 for rank in range(1, number_of + 1)]
    largest = reach if full else min(reach, max(-(-total // number_of), total * loads[0] // sum(loads)))
    least = 1 if total - largest >= number_of - 1 else 0
    given, rest = [largest] + [least] * (number_of - 1), total - largest - least * (number_of - 1)
    while rest > 0:
        free = [i for i in range(1, number_of) if given[i] < largest] or [i for i in range(1, number_of) if given[i] < reach]
        mass, remaining = sum([loads[i] for i in free]), rest
        for i in free:
            extra = min(reach - given[i], max(1, remaining * loads[i] // mass), rest)
            given[i] = given[i] + extra
            rest = rest - extra
    return np.array(given)


def noise(rng, extent, spread, most, cuts=(), kind=jnp.bfloat16):
    level = block_levels(rng, extent, cuts, -0.22, 0.18) if cuts else 1.0
    drawn = jax.random.normal(rng, extent, jnp.float32) * spread * level
    return jnp.minimum(jnp.maximum(drawn, -most), most).astype(kind)


def setup_inputs(seed: int = 0) -> dict:
    arg_keys = jax.random.split(jax.random.key(seed), 10)
    attn_heads = noise(arg_keys[0], (TOKENS, HEADS * HD), 1.0, 6.0, ((0, 64), (1, 4)))
    out_proj = noise(arg_keys[1], (HEADS * HD, D), (HEADS * HD) ** -0.5, 0.09375, ((0, 4), (1, 64)))
    residual = noise(arg_keys[2], (TOKENS, D), 1.0, 6.0, ((0, 64),))
    norm_gain = jnp.clip(1.0 + 0.18 * jax.random.normal(arg_keys[3], (D,), jnp.float32), 0.1, 1.9)
    route_ids_keys = jax.random.split(jax.random.fold_in(arg_keys[4], 1), TOKENS // TOK_DEV)
    route_ids_turns = jax.random.permutation(jax.random.fold_in(arg_keys[4], 3), TOKENS // TOK_DEV)
    route_ids = jax.vmap(lambda own, number: deal_out(jax.random.fold_in(arg_keys[4], 2), own, number, TOK_DEV, EXPERTS, TOP, CAP, 2))(route_ids_keys, route_ids_turns).reshape((TOKENS, TOP))
    route_weights = jnp.clip(jnp.exp(math.log(1.0) - 2.9957323 * jax.random.uniform(arg_keys[5], (TOKENS, TOP), jnp.float32) ** block_levels(arg_keys[5], (TOKENS, TOP), ((0, 64),), -0.2, 0.2)), 0.05, 1.0)
    w_gate = noise(arg_keys[6], (EXPERTS, D, FF), D ** -0.5, 0.09375, ((0, 64), (2, 4)))
    w_up = noise(arg_keys[7], (EXPERTS, D, FF), D ** -0.5, 0.09375, ((0, 64), (2, 4)))
    w_down = noise(arg_keys[8], (EXPERTS, FF, D), FF ** -0.5, 0.15625, ((0, 64), (1, 4)))
    return {"attn_heads": attn_heads, "out_proj": out_proj, "residual": residual, "norm_gain": norm_gain, "route_ids": route_ids, "route_weights": route_weights, "w_gate": w_gate, "w_up": w_up, "w_down": w_down}


def slot_places(ids):
    row_count, top_count = ids.shape
    onehot = (ids[:, :, None] == jnp.arange(EXPERTS, dtype=jnp.int32)[None, None, :]).astype(jnp.int32)
    flattened = onehot.reshape(row_count * top_count, EXPERTS)
    before = jnp.cumsum(flattened, axis=0).astype(jnp.int32) - flattened
    return lax.optimization_barrier(jnp.sum(before * flattened, axis=1)).astype(jnp.int32).reshape(row_count, top_count)

def reference(attn_heads, out_proj, residual, norm_gain, route_ids, route_weights, w_gate, w_up, w_down):
    attn_out = jnp.dot(attn_heads.astype(jnp.float32), out_proj.astype(jnp.float32))
    hidden = residual.astype(jnp.float32) + attn_out
    normed = (hidden * lax.rsqrt(lax.optimization_barrier(jnp.mean(hidden * hidden, axis=-1, keepdims=True)) + 1e-06) * norm_gain).astype(jnp.bfloat16)
    weights = route_weights / lax.optimization_barrier(jnp.sum(route_weights, axis=-1, keepdims=True))
    group_count = N_EXPERT
    slot_rank = jax.vmap(slot_places)(route_ids.reshape(group_count, TOK_DEV, TOP)).reshape(TOKENS, TOP)
    owner_group = (jnp.arange(TOKENS, dtype=jnp.int32) // TOK_DEV)[:, None]
    flat_index = ((route_ids * group_count + owner_group) * CAP + slot_rank).astype(jnp.int32).reshape(-1)
    token_ids = jnp.broadcast_to(jnp.arange(TOKENS, dtype=jnp.int32)[:, None], (TOKENS, TOP)).reshape(-1)
    slot_token = jnp.full((EXPERTS * group_count * CAP,), TOKENS, dtype=jnp.int32).at[flat_index].set(token_ids)
    slot_weight = jnp.zeros((EXPERTS * group_count * CAP,), jnp.float32).at[flat_index].set(weights.reshape(-1))
    slot_token = slot_token.reshape(EXPERTS, group_count * CAP)
    slot_weight = slot_weight.reshape(EXPERTS, group_count * CAP)
    padded = jnp.concatenate([normed, jnp.zeros((1, D), jnp.bfloat16)], axis=0)
    block_size = FF // N_TENSOR

    def per_expert(mixture, expert):
        chosen = slot_token[expert]
        inputs = padded[chosen].astype(jnp.float32)
        gate_acc = jnp.dot(inputs, w_gate[expert].astype(jnp.float32))
        upper = jnp.dot(inputs, w_up[expert].astype(jnp.float32))
        activation = (jax.nn.silu(gate_acc) * upper).astype(jnp.bfloat16).astype(jnp.float32)
        pieces = jnp.einsum('rtf,tfd->trd', activation.reshape(-1, N_TENSOR, block_size), w_down[expert].astype(jnp.float32).reshape(N_TENSOR, block_size, D))
        summed = lax.optimization_barrier(jnp.sum(pieces.astype(jnp.bfloat16).astype(jnp.float32), axis=0))
        rounded = summed.astype(jnp.bfloat16).astype(jnp.float32)
        mixture = mixture.at[chosen].add(slot_weight[expert][:, None] * rounded)
        return (mixture, None)
    mixture, ignored = lax.scan(per_expert, jnp.zeros((TOKENS + 1, D), jnp.float32), jnp.arange(EXPERTS, dtype=jnp.int32))
    return (hidden + mixture[:TOKENS]).astype(jnp.bfloat16)
```

```python
import jax
import jax.numpy as jnp
from jax import lax
from jax.sharding import PartitionSpec as P

EXPERTS = 64
MAIN = 16
OVER = 2
LANES = 128


def routing(route_ids, route_weights):
    count = route_ids.shape[0]
    hits = (route_ids[:, :, None] == jnp.arange(EXPERTS, dtype=jnp.int32)[None, None, :]).astype(
        jnp.float32
    )
    chosen = jnp.sum(hits, axis=1)
    weights = route_weights / jnp.sum(route_weights, axis=-1, keepdims=True)
    weight = jnp.sum(hits * weights[:, :, None], axis=1)
    order = jnp.arange(count, dtype=jnp.int32)
    earlier = (order[None, :] < order[:, None]).astype(jnp.bfloat16)
    rank = jnp.dot(earlier, chosen.astype(jnp.bfloat16), preferred_element_type=jnp.float32)
    rank = jnp.where(chosen > 0, rank, -1.0)
    return rank.astype(jnp.int32), weight


def per_device(
    attn_heads, out_proj, residual, norm_gain, route_ids, route_weights, w_gate, w_up, w_down
):
    tokens, model_width = residual.shape
    members = lax.axis_size("tensor")
    member = lax.axis_index("tensor")
    cols = model_width // members
    groups = cols // LANES
    rows = EXPERTS * MAIN

    rank, weight = routing(route_ids, route_weights)
    row = jnp.arange(rows, dtype=jnp.int32)
    slot = row % MAIN
    spread = jnp.repeat(rank, MAIN, axis=1)
    main_hit = spread == slot[None, :]
    over_hit = spread == (MAIN + slot // groups)[None, :]
    row_weight = jnp.repeat(weight, MAIN, axis=1)

    heads_out = jnp.dot(
        attn_heads,
        lax.all_gather(out_proj, "expert", axis=1, tiled=True),
        preferred_element_type=jnp.float32,
    ).astype(jnp.bfloat16)
    attn_out = lax.psum_scatter(
        jnp.transpose(heads_out.reshape(tokens, members, cols), (1, 0, 2)),
        "tensor",
        scatter_dimension=0,
        tiled=True,
    )[0].astype(jnp.float32)
    own_residual = lax.dynamic_slice_in_dim(residual, member * cols, cols, 1)
    own_gain = lax.dynamic_slice_in_dim(norm_gain, member * cols, cols, 0)
    hidden = own_residual.astype(jnp.float32) + attn_out
    squares = lax.psum(jnp.sum(hidden * hidden, axis=-1, keepdims=True), "tensor")
    normed = (hidden * lax.rsqrt(squares / model_width + 1e-06) * own_gain).astype(jnp.bfloat16)

    main = jnp.einsum(
        "tr,td->rd", main_hit.astype(jnp.bfloat16), normed, preferred_element_type=jnp.float32
    ).astype(jnp.bfloat16)
    wide = jnp.einsum(
        "tr,td->rd", over_hit.astype(jnp.bfloat16), normed, preferred_element_type=jnp.float32
    ).astype(jnp.bfloat16)
    own_group = (row % groups)[:, None]
    over = jnp.zeros((rows, LANES), jnp.bfloat16)
    for g in range(groups):
        over = jnp.where(own_group == g, wide[:, g * LANES : (g + 1) * LANES], over)
    packed = jnp.concatenate([main, over], axis=1).reshape(EXPERTS, MAIN, cols + LANES)
    arrived = lax.all_to_all(packed, "expert", split_axis=0, concat_axis=0, tiled=True)
    full = lax.all_gather(arrived.reshape(rows, cols + LANES), "tensor", axis=0)
    main_in = jnp.concatenate([full[m, :, :cols] for m in range(members)], axis=1)
    over_in = jnp.transpose(
        full[:, :, cols:].reshape(members, EXPERTS * OVER, groups, LANES), (1, 0, 2, 3)
    ).reshape(EXPERTS * OVER, model_width)
    inputs = jnp.concatenate([main_in, over_in], axis=0)
    gate = jnp.dot(inputs, w_gate[0], preferred_element_type=jnp.float32)
    up = jnp.dot(inputs, w_up[0], preferred_element_type=jnp.float32)
    act = (jax.nn.silu(gate) * up).astype(jnp.bfloat16)
    down = w_down[0].reshape(-1, members, cols)
    parts = jnp.stack(
        [jnp.dot(act, down[:, m], preferred_element_type=jnp.float32) for m in range(members)]
    ).astype(jnp.bfloat16)
    summed = lax.psum_scatter(parts, "tensor", scatter_dimension=0, tiled=True)[0]
    back = jnp.concatenate(
        [summed[:rows], summed[rows:].reshape(rows, LANES)], axis=1
    ).reshape(EXPERTS, MAIN, cols + LANES)
    returned = lax.all_to_all(back, "expert", split_axis=0, concat_axis=0, tiled=True).reshape(
        rows, cols + LANES
    )
    high = row_weight.astype(jnp.bfloat16)
    low = (row_weight - high.astype(jnp.float32)).astype(jnp.bfloat16)
    mixture = 0.0
    zero = jnp.zeros((), jnp.bfloat16)
    for part in (high, low):
        pick = jnp.where(main_hit, part, zero)
        mixture += jnp.dot(pick, returned[:, :cols], preferred_element_type=jnp.float32)
        extra = [
            jnp.dot(
                jnp.where(over_hit & (row % groups == g)[None, :], part, zero),
                returned[:, cols:],
                preferred_element_type=jnp.float32,
            )
            for g in range(groups)
        ]
        mixture += jnp.concatenate(extra, axis=1)
    return (hidden + mixture).astype(jnp.bfloat16)


def solution(mesh):
    placed = (
        P("expert", "tensor"),
        P("tensor", "expert"),
        P("expert", None),
        P(),
        P("expert", None),
        P("expert", None),
        P("expert", None, "tensor"),
        P("expert", None, "tensor"),
        P("expert", "tensor", None),
    )
    return jax.shard_map(
        per_device, mesh=mesh, in_specs=placed, out_specs=P("expert", "tensor"), check_vma=False
    )
```

```python
import jax
import jax.numpy as jnp
import numpy as np
from jax import lax
from jax.experimental import pallas as pl
from jax.experimental.pallas import tpu as pltpu
from jax.sharding import PartitionSpec as P

MESH = pl.DeviceIdType.MESH
EXPERTS = 64
RING = 16
ROWS_Y = EXPERTS // RING
MAIN = 16
OVER = 2
LANES = 128
CHUNKS = 4
PER = EXPERTS // CHUNKS
CHUNK_MAIN = PER * MAIN
CHUNK_OVER = PER * OVER
CHUNK_ROWS = CHUNK_MAIN + CHUNK_OVER
HALF_IN = CHUNK_MAIN // 2
HALF_OUT = CHUNK_ROWS // 2 // 16 * 16


def routing(ids, route_weights):
    count = ids.shape[0]
    hits = (ids[:, :, None] == jnp.arange(EXPERTS, dtype=jnp.int32)[None, None, :]).astype(
        jnp.float32
    )
    chosen = jnp.sum(hits, axis=1)
    weights = route_weights / jnp.sum(route_weights, axis=-1, keepdims=True)
    weight = jnp.sum(hits * weights[:, :, None], axis=1)
    order = jnp.arange(count, dtype=jnp.int32)
    earlier = (order[None, :] < order[:, None]).astype(jnp.bfloat16)
    rank = jnp.dot(earlier, chosen.astype(jnp.bfloat16), preferred_element_type=jnp.float32)
    rank = jnp.where(chosen > 0, rank, -1.0)
    return rank.astype(jnp.int32), weight


def overflow_order():
    groups = MAIN // OVER
    matrix = np.zeros((CHUNK_MAIN, CHUNK_MAIN), np.float32)
    for g in range(groups):
        for s in range(PER):
            for c in range(OVER):
                matrix[g * CHUNK_OVER + s * OVER + c, s * MAIN + c * groups + g] = 1.0
    return matrix


def expert_kernel(
    packed, gate_hbm, up_hbm, down_hbm, sort, unsort, back,
    inbox, gate_up, down, acc, to_right, to_left, to_far, own,
    far_a, far_b, from_left, from_right, outbox,
    weight_sem, local_sem, dsend, drecv, asend, arecv, rsend, rrecv, bsend, brecv,
):
    me = lax.axis_index("expert")
    x = lax.axis_index("tensor")
    y, zc = lax.div(me, RING), lax.rem(me, RING)
    right, left, far = lax.rem(x + 1, 4), lax.rem(x + 3, 4), lax.rem(x + 2, 4)
    ff = gate_hbm.shape[1]
    cols = packed.shape[1] - LANES
    groups = cols // LANES

    def ahead(k):
        return lax.rem(y + lax.div(k, RING), ROWS_Y) * RING + lax.rem(zc + lax.rem(k, RING), RING)

    def behind(k):
        return lax.rem(y + ROWS_Y - lax.div(k, RING), ROWS_Y) * RING + lax.rem(
            zc + RING - lax.rem(k, RING), RING
        )

    weights = [
        pltpu.make_async_copy(gate_hbm, gate_up.at[:, pl.ds(0, ff)], weight_sem.at[0]),
        pltpu.make_async_copy(up_hbm, gate_up.at[:, pl.ds(ff, ff)], weight_sem.at[1]),
        pltpu.make_async_copy(down_hbm, down, weight_sem.at[2]),
    ]
    for copy in weights:
        copy.start()

    barrier = pltpu.get_barrier_semaphore()

    @pl.loop(1, EXPERTS)
    def _(k):
        pl.semaphore_signal(barrier, inc=1, device_id=(ahead(k), x), device_id_type=MESH)

    for m in (right, left):
        pl.semaphore_signal(barrier, inc=1, device_id=(me, m), device_id_type=MESH)
    pl.semaphore_wait(barrier, EXPERTS + 1)

    def block(k):
        return pl.ds(pl.multiple_of(k * MAIN, MAIN), MAIN)

    def dispatch(k):
        return pltpu.make_async_remote_copy(
            src_ref=packed.at[block(k)],
            dst_ref=inbox.at[lax.div(k, PER), x, block(lax.rem(k, PER))],
            send_sem=dsend.at[k],
            recv_sem=drecv.at[k],
            device_id=(ahead(k), x),
            device_id_type=MESH,
        )

    own_in = pltpu.make_async_copy(
        packed.at[pl.ds(0, MAIN)], inbox.at[0, x, pl.ds(0, MAIN)], local_sem.at[0]
    )
    own_in.start()

    @pl.loop(1, EXPERTS)
    def _(k):
        dispatch(k).start()

    own_in.wait()

    low, high = pl.ds(0, HALF_IN), pl.ds(HALF_IN, HALF_IN)

    def gather(c, i):
        owner = (x, x, x, x, left, right)[i]
        part = (low, high, high, low, low, high)[i]
        target = (right, right, left, left, right, left)[i]
        ref = inbox.at[c, owner, part]
        return pltpu.make_async_remote_copy(
            src_ref=ref,
            dst_ref=ref,
            send_sem=asend.at[c, i],
            recv_sem=arecv.at[c, i],
            device_id=(me, target),
            device_id_type=MESH,
        )

    head, tail = pl.ds(0, HALF_OUT), pl.ds(HALF_OUT, CHUNK_ROWS - HALF_OUT)

    def reduce(c, i):
        source = (to_far.at[c, head], to_far.at[c, tail], to_right.at[c], to_left.at[c])[i]
        landing = (far_a.at[c], far_b.at[c], from_left.at[c], from_right.at[c])[i]
        target = (right, left, right, left)[i]
        return pltpu.make_async_remote_copy(
            src_ref=source,
            dst_ref=landing,
            send_sem=rsend.at[c, i],
            recv_sem=rrecv.at[c, i],
            device_id=(me, target),
            device_id_type=MESH,
        )

    def give_back(k):
        return pltpu.make_async_remote_copy(
            src_ref=outbox.at[lax.div(k, PER), block(lax.rem(k, PER))],
            dst_ref=back.at[block(k)],
            send_sem=bsend.at[k],
            recv_sem=brecv.at[k],
            device_id=(behind(k), x),
            device_id_type=MESH,
        )

    own_out = pltpu.make_async_copy(
        outbox.at[0, pl.ds(0, MAIN)], back.at[pl.ds(0, MAIN)], local_sem.at[1]
    )

    def project(act, quarter):
        columns = pl.ds(pl.multiple_of(quarter * cols, cols), cols)
        return jnp.dot(act, down[:, columns], preferred_element_type=jnp.float32)

    def compute(c):
        tails = jnp.concatenate([inbox[c, m, :, cols:] for m in range(4)], axis=1)
        tails = jnp.dot(sort[...], tails, preferred_element_type=jnp.float32).astype(jnp.bfloat16)
        for m in range(4):
            extra = jnp.concatenate(
                [
                    tails[g * CHUNK_OVER : (g + 1) * CHUNK_OVER, m * LANES : (m + 1) * LANES]
                    for g in range(groups)
                ],
                axis=1,
            )
            rows = jnp.concatenate([inbox[c, m, :, :cols], extra], axis=0)
            part = jnp.dot(
                rows, gate_up[m * cols : (m + 1) * cols, :], preferred_element_type=jnp.float32
            )
            if m == 0:
                acc[...] = part
            else:
                acc[...] += part
        gate, up = acc[:, :ff], acc[:, ff:]
        act = (gate / (1.0 + jnp.exp(-gate)) * up).astype(jnp.bfloat16)
        to_far[c] = project(act, far).astype(jnp.bfloat16)
        reduce(c, 0).start()
        reduce(c, 1).start()
        to_right[c] = project(act, right).astype(jnp.bfloat16)
        to_left[c] = project(act, left).astype(jnp.bfloat16)
        own[c] = project(act, x)

    @pl.loop(0, CHUNKS + 4)
    def _(t):
        @pl.when(t < CHUNKS)
        def _():
            @pl.loop(0, PER)
            def _(j):
                @pl.when(t * PER + j > 0)
                def _():
                    dispatch(t * PER + j).wait_recv()

            for i in (0, 2, 1, 3):
                gather(t, i).start()

        @pl.when((t >= 1) & (t < CHUNKS + 1))
        def _():
            c = t - 1
            gather(c, 0).wait_recv()
            gather(c, 4).start()
            gather(c, 2).wait_recv()
            gather(c, 5).start()

        @pl.when(t == 2)
        def _():
            for copy in weights:
                copy.wait()

        @pl.when((t >= 2) & (t < CHUNKS + 2))
        def _():
            c = t - 2
            for i in (1, 3, 4, 5):
                gather(c, i).wait_recv()
            compute(c)

        @pl.when((t >= 3) & (t < CHUNKS + 3))
        def _():
            c = t - 3
            reduce(c, 0).wait_recv()
            to_right[c, :HALF_OUT] = (
                to_right[c, :HALF_OUT].astype(jnp.float32) + far_a[c].astype(jnp.float32)
            ).astype(jnp.bfloat16)
            reduce(c, 2).start()
            reduce(c, 1).wait_recv()
            to_left[c, HALF_OUT:] = (
                to_left[c, HALF_OUT:].astype(jnp.float32) + far_b[c].astype(jnp.float32)
            ).astype(jnp.bfloat16)
            reduce(c, 3).start()

        @pl.when(t >= 4)
        def _():
            c = t - 4
            reduce(c, 2).wait_recv()
            reduce(c, 3).wait_recv()
            total = (
                own[c] + from_left[c].astype(jnp.float32) + from_right[c].astype(jnp.float32)
            ).astype(jnp.bfloat16)
            outbox[c, :, :cols] = total[:CHUNK_MAIN]
            extra = jnp.concatenate(
                [total[CHUNK_MAIN:, g * LANES : (g + 1) * LANES] for g in range(groups)], axis=0
            )
            outbox[c, :, cols:] = jnp.dot(
                unsort[...], extra, preferred_element_type=jnp.float32
            ).astype(jnp.bfloat16)

            @pl.when(c == 0)
            def _():
                own_out.start()

            @pl.loop(0, PER)
            def _(j):
                @pl.when(c * PER + j > 0)
                def _():
                    give_back(c * PER + j).start()

    own_out.wait()

    @pl.loop(1, EXPERTS)
    def _(k):
        give_back(k).wait_recv()

    @pl.loop(1, EXPERTS)
    def _(k):
        dispatch(k).wait_send()
        give_back(k).wait_send()

    @pl.loop(0, CHUNKS)
    def _(c):
        for i in range(6):
            gather(c, i).wait_send()
        for i in range(4):
            reduce(c, i).wait_send()


def experts(packed, w_gate, w_up, w_down):
    width = packed.shape[1]
    cols = width - LANES
    ff, model_width = w_down.shape
    order = overflow_order()
    rows = CHUNK_ROWS
    bf16, f32 = jnp.bfloat16, jnp.float32
    dma = pltpu.SemaphoreType.DMA
    anywhere = pl.BlockSpec(memory_space=pl.ANY)
    onchip = pl.BlockSpec(memory_space=pltpu.VMEM)
    return pl.pallas_call(
        expert_kernel,
        out_shape=jax.ShapeDtypeStruct(packed.shape, bf16),
        in_specs=[anywhere] * 4 + [onchip] * 2,
        out_specs=anywhere,
        scratch_shapes=[
            pltpu.VMEM((CHUNKS, 4, CHUNK_MAIN, width), bf16),
            pltpu.VMEM((model_width, 2 * ff), bf16),
            pltpu.VMEM((ff, model_width), bf16),
            pltpu.VMEM((rows, 2 * ff), f32),
            pltpu.VMEM((CHUNKS, rows, cols), bf16),
            pltpu.VMEM((CHUNKS, rows, cols), bf16),
            pltpu.VMEM((CHUNKS, rows, cols), bf16),
            pltpu.VMEM((CHUNKS, rows, cols), f32),
            pltpu.VMEM((CHUNKS, HALF_OUT, cols), bf16),
            pltpu.VMEM((CHUNKS, rows - HALF_OUT, cols), bf16),
            pltpu.VMEM((CHUNKS, rows, cols), bf16),
            pltpu.VMEM((CHUNKS, rows, cols), bf16),
            pltpu.VMEM((CHUNKS, CHUNK_MAIN, width), bf16),
            dma((3,)),
            dma((2,)),
            dma((EXPERTS,)),
            dma((EXPERTS,)),
            dma((CHUNKS, 6)),
            dma((CHUNKS, 6)),
            dma((CHUNKS, 4)),
            dma((CHUNKS, 4)),
            dma((EXPERTS,)),
            dma((EXPERTS,)),
        ],
        compiler_params=pltpu.CompilerParams(
            collective_id=1, has_side_effects=True, vmem_limit_bytes=58 << 20
        ),
    )(packed, w_gate, w_up, w_down, jnp.asarray(order, bf16), jnp.asarray(order.T, bf16))


def per_device(
    attn_heads, out_proj, residual, norm_gain, route_ids, route_weights, w_gate, w_up, w_down
):
    tokens, model_width = residual.shape
    members = lax.axis_size("tensor")
    member = lax.axis_index("tensor")
    place = lax.axis_index("expert")
    cols = model_width // members
    groups = cols // LANES
    rows = EXPERTS * MAIN

    relative = ((route_ids // RING - place // RING) % ROWS_Y) * RING + (
        route_ids % RING - place % RING
    ) % RING
    rank, weight = routing(relative, route_weights)
    row = jnp.arange(rows, dtype=jnp.int32)
    slot = row % MAIN
    spread = jnp.repeat(rank, MAIN, axis=1)
    main_hit = spread == slot[None, :]
    over_hit = spread == (MAIN + slot // groups)[None, :]
    row_weight = jnp.repeat(weight, MAIN, axis=1)

    heads_out = jnp.dot(
        attn_heads,
        lax.all_gather(out_proj, "expert", axis=1, tiled=True),
        preferred_element_type=jnp.float32,
    ).astype(jnp.bfloat16)
    attn_out = lax.psum_scatter(
        jnp.transpose(heads_out.reshape(tokens, members, cols), (1, 0, 2)),
        "tensor",
        scatter_dimension=0,
        tiled=True,
    )[0].astype(jnp.float32)
    own_residual = lax.dynamic_slice_in_dim(residual, member * cols, cols, 1)
    own_gain = lax.dynamic_slice_in_dim(norm_gain, member * cols, cols, 0)
    hidden = own_residual.astype(jnp.float32) + attn_out
    squares = lax.psum(jnp.sum(hidden * hidden, axis=-1, keepdims=True), "tensor")
    normed = (hidden * lax.rsqrt(squares / model_width + 1e-06) * own_gain).astype(jnp.bfloat16)

    main = jnp.einsum(
        "tr,td->rd", main_hit.astype(jnp.bfloat16), normed, preferred_element_type=jnp.float32
    ).astype(jnp.bfloat16)
    wide = jnp.einsum(
        "tr,td->rd", over_hit.astype(jnp.bfloat16), normed, preferred_element_type=jnp.float32
    ).astype(jnp.bfloat16)
    own_group = (row % groups)[:, None]
    over = jnp.zeros((rows, LANES), jnp.bfloat16)
    for g in range(groups):
        over = jnp.where(own_group == g, wide[:, g * LANES : (g + 1) * LANES], over)
    packed = jnp.concatenate([main, over], axis=1)
    returned = experts(packed, w_gate[0], w_up[0], w_down[0])
    high = row_weight.astype(jnp.bfloat16)
    low = (row_weight - high.astype(jnp.float32)).astype(jnp.bfloat16)
    mixture = 0.0
    zero = jnp.zeros((), jnp.bfloat16)
    for part in (high, low):
        pick = jnp.where(main_hit, part, zero)
        mixture += jnp.dot(pick, returned[:, :cols], preferred_element_type=jnp.float32)
        extra = [
            jnp.dot(
                jnp.where(over_hit & (row % groups == g)[None, :], part, zero),
                returned[:, cols:],
                preferred_element_type=jnp.float32,
            )
            for g in range(groups)
        ]
        mixture += jnp.concatenate(extra, axis=1)
    return (hidden + mixture).astype(jnp.bfloat16)


def solution(mesh):
    placed = (
        P("expert", "tensor"),
        P("tensor", "expert"),
        P("expert", None),
        P(),
        P("expert", None),
        P("expert", None),
        P("expert", None, "tensor"),
        P("expert", None, "tensor"),
        P("expert", "tensor", None),
    )
    return jax.shard_map(
        per_device, mesh=mesh, in_specs=placed, out_specs=P("expert", "tensor"), check_vma=False
    )
```

```python
import jax
import jax.numpy as jnp
import numpy as np
from jax import lax
from jax.experimental import pallas as pl
from jax.experimental.pallas import tpu as pltpu
from jax.sharding import PartitionSpec as P

MESH = pl.DeviceIdType.MESH
EXPERTS = 64
RING = 16
ROWS_Y = EXPERTS // RING
MAIN = 16
OVER = 2
LANES = 128
CHUNKS = 4
PER = EXPERTS // CHUNKS
CHUNK_MAIN = PER * MAIN
CHUNK_OVER = PER * OVER
CHUNK_ROWS = CHUNK_MAIN + CHUNK_OVER
HALF_IN = CHUNK_MAIN // 2
HALF_OUT = CHUNK_ROWS // 2 // 16 * 16


def routing(ids, route_weights):
    count = ids.shape[0]
    hits = (ids[:, :, None] == jnp.arange(EXPERTS, dtype=jnp.int32)[None, None, :]).astype(
        jnp.float32
    )
    chosen = jnp.sum(hits, axis=1)
    weights = route_weights / jnp.sum(route_weights, axis=-1, keepdims=True)
    weight = jnp.sum(hits * weights[:, :, None], axis=1)
    order = jnp.arange(count, dtype=jnp.int32)
    earlier = (order[None, :] < order[:, None]).astype(jnp.bfloat16)
    rank = jnp.dot(earlier, chosen.astype(jnp.bfloat16), preferred_element_type=jnp.float32)
    rank = jnp.where(chosen > 0, rank, -1.0)
    return rank.astype(jnp.int32), weight


def overflow_order():
    groups = MAIN // OVER
    matrix = np.zeros((CHUNK_MAIN, CHUNK_MAIN), np.float32)
    for g in range(groups):
        for s in range(PER):
            for c in range(OVER):
                matrix[g * CHUNK_OVER + s * OVER + c, s * MAIN + c * groups + g] = 1.0
    return matrix


def attention_kernel(
    heads_hbm, proj_hbm, residual_hbm, gain_hbm, hidden_out, normed_out,
    shard, sibling_shard, weight, heads, to_far, to_right, to_left, own,
    far_a, far_b, from_left, from_right, mine, arrived, residual, gain, squares,
    local_sem, shard_sem, zsend, zrecv, csend, crecv, hsend, hrecv, rsend, rrecv, wsem, nsend, nrecv,
):
    me = lax.axis_index("expert")
    x = lax.axis_index("tensor")
    y, zc = lax.div(me, RING), lax.rem(me, RING)
    core, z = lax.rem(zc, 2), lax.div(zc, 2)
    depth = RING // 2
    right, left, far = lax.rem(x + 1, 4), lax.rem(x + 3, 4), lax.rem(x + 2, 4)
    sibling = me + 1 - 2 * core
    cols = weight.shape[1]
    half = weight.shape[0] // 2
    tokens = heads.shape[1]

    def along_z(step):
        return y * RING + lax.rem(z + depth + step, depth) * 2 + core

    def along_y(step):
        return lax.rem(y + step, ROWS_Y) * RING + zc

    partner = (x * RING + zc, y)
    local = [
        pltpu.make_async_copy(proj_hbm, shard, local_sem.at[0]),
        pltpu.make_async_copy(heads_hbm, heads.at[y], local_sem.at[1]),
        pltpu.make_async_copy(
            residual_hbm.at[:, pl.ds(pl.multiple_of(x * cols, cols), cols)], residual, local_sem.at[2]
        ),
        pltpu.make_async_copy(
            gain_hbm.at[:, pl.ds(pl.multiple_of(x * cols, cols), cols)], gain, local_sem.at[3]
        ),
    ]
    for copy in local:
        copy.start()

    barrier = pltpu.get_barrier_semaphore()
    for device in (sibling, along_z(1), along_z(-1), along_y(1), along_y(2), along_y(3)):
        pl.semaphore_signal(barrier, inc=1, device_id=(device, x), device_id_type=MESH)
    for m in (right, left, far):
        pl.semaphore_signal(barrier, inc=1, device_id=(me, m), device_id_type=MESH)

    @pl.when(x != y)
    def _():
        pl.semaphore_signal(barrier, inc=1, device_id=partner, device_id_type=MESH)
        pl.semaphore_wait(barrier, 10)

    @pl.when(x == y)
    def _():
        pl.semaphore_wait(barrier, 9)

    def remote(source, landing, send, recv, device):
        return pltpu.make_async_remote_copy(
            src_ref=source,
            dst_ref=landing,
            send_sem=send,
            recv_sem=recv,
            device_id=device,
            device_id_type=MESH,
        )

    swap_shard = remote(
        shard.at[pl.ds(pl.multiple_of((1 - core) * half, half), half)],
        sibling_shard,
        shard_sem.at[0],
        shard_sem.at[1],
        (sibling, x),
    )
    local[0].wait()
    swap_shard.start()
    local[1].wait()

    def share_heads(i):
        return remote(heads.at[y], heads.at[y], hsend.at[i], hrecv.at[i], (along_y(i + 1), x))

    for i in (1, 0, 2):
        share_heads(i).start()

    def piece(owner, part):
        start = core * half + (half // 2 if part == 2 else 0)
        count = half if part == 0 else half // 2
        return weight.at[
            pl.ds(pl.multiple_of(start, half // 2), count),
            pl.ds(pl.multiple_of(owner * LANES, LANES), LANES),
        ]

    def ring(direction, s):
        offset = -(s - 1) if direction == 0 else s - 1
        ref = piece(
            lax.rem(z + depth + offset, depth), (1 + direction) if s == depth // 2 else 0
        )
        target = along_z(1 if direction == 0 else -1)
        return remote(ref, ref, zsend.at[direction, s - 1], zrecv.at[direction, s - 1], (target, x))

    def across(direction, s):
        offset = -s if direction == 0 else s
        ref = piece(
            lax.rem(z + depth + offset, depth), (1 + direction) if s == depth // 2 else 0
        )
        i = 5 * direction + s
        return remote(ref, ref, csend.at[i], crecv.at[i], (sibling, x))

    width = shard.shape[1]
    row = lax.broadcasted_iota(jnp.int32, (width, LANES), 0)
    lane = lax.broadcasted_iota(jnp.int32, (width, LANES), 1)
    put_own = (lane == row + width * core).astype(jnp.bfloat16)
    put_other = (lane == row + width * (1 - core)).astype(jnp.bfloat16)
    swap_shard.wait_recv()
    both = jnp.dot(
        shard[pl.ds(pl.multiple_of(core * half, half), half), :],
        put_own,
        preferred_element_type=jnp.float32,
    ) + jnp.dot(sibling_shard[...], put_other, preferred_element_type=jnp.float32)
    weight[
        pl.ds(pl.multiple_of(core * half, half), half),
        pl.ds(pl.multiple_of(z * LANES, LANES), LANES),
    ] = both.astype(jnp.bfloat16)
    ring(0, 1).start()
    ring(1, 1).start()
    across(0, 0).start()
    for s in range(1, depth // 2 + 1):
        for direction in (0, 1):
            ring(direction, s).wait_recv()
            if s < depth // 2:
                ring(direction, s + 1).start()
            across(direction, s).start()
    handed = [(0, 0)] + [(d, s) for s in range(1, depth // 2 + 1) for d in (0, 1)]
    for i in (0, 2, 1):
        share_heads(i).wait_recv()
    for d, s in handed:
        across(d, s).wait_recv()

    def partial(block):
        return jnp.dot(heads[block], weight[...], preferred_element_type=jnp.float32)

    part = tokens // 2

    def reduce(i):
        source = (to_far.at[pl.ds(0, part)], to_far.at[pl.ds(part, part)], to_right, to_left)[i]
        landing = (far_a, far_b, from_left, from_right)[i]
        target = (right, left, right, left)[i]
        return remote(source, landing, rsend.at[i], rrecv.at[i], (me, target))

    to_far[...] = partial(far).astype(jnp.bfloat16)
    reduce(0).start()
    reduce(1).start()
    via_right = partial(right)
    reduce(0).wait_recv()
    to_right[:part] = (via_right[:part] + far_a[...].astype(jnp.float32)).astype(jnp.bfloat16)
    to_right[part:] = via_right[part:].astype(jnp.bfloat16)
    reduce(2).start()
    via_left = partial(left)
    reduce(1).wait_recv()
    to_left[:part] = via_left[:part].astype(jnp.bfloat16)
    to_left[part:] = (via_left[part:] + far_b[...].astype(jnp.float32)).astype(jnp.bfloat16)
    reduce(3).start()
    own[...] = partial(x)
    reduce(2).wait_recv()
    reduce(3).wait_recv()
    mine[...] = (
        own[...] + from_left[...].astype(jnp.float32) + from_right[...].astype(jnp.float32)
    ).astype(jnp.bfloat16)
    exchange = remote(mine, arrived, wsem.at[0], wsem.at[1], partner)

    @pl.when(x != y)
    def _():
        exchange.start()
        exchange.wait_recv()
        exchange.wait_send()

    @pl.when(x == y)
    def _():
        arrived[...] = mine[...]

    local[2].wait()
    local[3].wait()
    hidden = residual[...].astype(jnp.float32) + arrived[...].astype(jnp.float32)
    hidden_out[...] = hidden
    squares[0] = jnp.broadcast_to(
        jnp.sum(hidden * hidden, axis=-1, keepdims=True), (tokens, LANES)
    )

    def share_squares(i):
        return remote(
            squares.at[0], squares.at[i + 1], nsend.at[i], nrecv.at[i], (me, (right, far, left)[i])
        )

    for i in range(3):
        share_squares(i).start()
    for i in range(3):
        share_squares(i).wait_recv()
    mean = (squares[0] + squares[1] + squares[2] + squares[3]) / (4 * cols)
    scale = lax.rsqrt(mean + 1e-06)[:, :1]
    normed_out[...] = (hidden * scale * gain[...]).astype(jnp.bfloat16)

    swap_shard.wait_send()
    for i in range(3):
        share_heads(i).wait_send()
        share_squares(i).wait_send()
    for d, s in handed:
        across(d, s).wait_send()
    for s in range(1, depth // 2 + 1):
        for direction in (0, 1):
            ring(direction, s).wait_send()
    for i in range(4):
        reduce(i).wait_send()


def attention(attn_heads, out_proj, residual, norm_gain):
    tokens, depth = attn_heads.shape
    cols = residual.shape[1] // 4
    bf16, f32 = jnp.bfloat16, jnp.float32
    dma = pltpu.SemaphoreType.DMA
    anywhere = pl.BlockSpec(memory_space=pl.ANY)
    onchip = pl.BlockSpec(memory_space=pltpu.VMEM)
    block = pltpu.VMEM((tokens, cols), bf16)
    return pl.pallas_call(
        attention_kernel,
        out_shape=(
            jax.ShapeDtypeStruct((tokens, cols), f32),
            jax.ShapeDtypeStruct((tokens, cols), bf16),
        ),
        in_specs=[anywhere] * 4,
        out_specs=(onchip, onchip),
        scratch_shapes=[
            pltpu.VMEM(out_proj.shape, bf16),
            pltpu.VMEM((depth // 2, out_proj.shape[1]), bf16),
            pltpu.VMEM((depth, cols), bf16),
            pltpu.VMEM((ROWS_Y, tokens, depth), bf16),
            block,
            block,
            block,
            pltpu.VMEM((tokens, cols), f32),
            pltpu.VMEM((tokens // 2, cols), bf16),
            pltpu.VMEM((tokens // 2, cols), bf16),
            block,
            block,
            block,
            block,
            block,
            pltpu.VMEM((1, cols), f32),
            pltpu.VMEM((4, tokens, LANES), f32),
            dma((4,)),
            dma((2,)),
            dma((2, 4)),
            dma((2, 4)),
            dma((10,)),
            dma((10,)),
            dma((3,)),
            dma((3,)),
            dma((4,)),
            dma((4,)),
            dma((2,)),
            dma((3,)),
            dma((3,)),
        ],
        compiler_params=pltpu.CompilerParams(
            collective_id=2, has_side_effects=True, vmem_limit_bytes=32 << 20
        ),
    )(attn_heads, out_proj, residual, norm_gain[None, :])


def expert_kernel(
    packed, gate_hbm, up_hbm, down_hbm, sort, unsort, back,
    inbox, gate_up, down, acc, to_right, to_left, to_far, own,
    far_a, far_b, from_left, from_right, outbox,
    weight_sem, local_sem, dsend, drecv, asend, arecv, rsend, rrecv, bsend, brecv,
):
    me = lax.axis_index("expert")
    x = lax.axis_index("tensor")
    y, zc = lax.div(me, RING), lax.rem(me, RING)
    right, left, far = lax.rem(x + 1, 4), lax.rem(x + 3, 4), lax.rem(x + 2, 4)
    ff = gate_hbm.shape[1]
    cols = packed.shape[1] - LANES
    groups = cols // LANES

    def ahead(k):
        return lax.rem(y + lax.div(k, RING), ROWS_Y) * RING + lax.rem(zc + lax.rem(k, RING), RING)

    def behind(k):
        return lax.rem(y + ROWS_Y - lax.div(k, RING), ROWS_Y) * RING + lax.rem(
            zc + RING - lax.rem(k, RING), RING
        )

    weights = [
        pltpu.make_async_copy(gate_hbm, gate_up.at[:, pl.ds(0, ff)], weight_sem.at[0]),
        pltpu.make_async_copy(up_hbm, gate_up.at[:, pl.ds(ff, ff)], weight_sem.at[1]),
        pltpu.make_async_copy(down_hbm, down, weight_sem.at[2]),
    ]
    for copy in weights:
        copy.start()

    barrier = pltpu.get_barrier_semaphore()

    @pl.loop(1, EXPERTS)
    def _(k):
        pl.semaphore_signal(barrier, inc=1, device_id=(ahead(k), x), device_id_type=MESH)

    for m in (right, left):
        pl.semaphore_signal(barrier, inc=1, device_id=(me, m), device_id_type=MESH)
    pl.semaphore_wait(barrier, EXPERTS + 1)

    def block(k):
        return pl.ds(pl.multiple_of(k * MAIN, MAIN), MAIN)

    def dispatch(k):
        return pltpu.make_async_remote_copy(
            src_ref=packed.at[block(k)],
            dst_ref=inbox.at[lax.div(k, PER), x, block(lax.rem(k, PER))],
            send_sem=dsend.at[k],
            recv_sem=drecv.at[k],
            device_id=(ahead(k), x),
            device_id_type=MESH,
        )

    own_in = pltpu.make_async_copy(
        packed.at[pl.ds(0, MAIN)], inbox.at[0, x, pl.ds(0, MAIN)], local_sem.at[0]
    )
    own_in.start()

    @pl.loop(1, EXPERTS)
    def _(k):
        dispatch(k).start()

    own_in.wait()

    low, high = pl.ds(0, HALF_IN), pl.ds(HALF_IN, HALF_IN)

    def gather(c, i):
        owner = (x, x, x, x, left, right)[i]
        part = (low, high, high, low, low, high)[i]
        target = (right, right, left, left, right, left)[i]
        ref = inbox.at[c, owner, part]
        return pltpu.make_async_remote_copy(
            src_ref=ref,
            dst_ref=ref,
            send_sem=asend.at[c, i],
            recv_sem=arecv.at[c, i],
            device_id=(me, target),
            device_id_type=MESH,
        )

    head, tail = pl.ds(0, HALF_OUT), pl.ds(HALF_OUT, CHUNK_ROWS - HALF_OUT)

    def reduce(c, i):
        source = (to_far.at[c, head], to_far.at[c, tail], to_right.at[c], to_left.at[c])[i]
        landing = (far_a.at[c], far_b.at[c], from_left.at[c], from_right.at[c])[i]
        target = (right, left, right, left)[i]
        return pltpu.make_async_remote_copy(
            src_ref=source,
            dst_ref=landing,
            send_sem=rsend.at[c, i],
            recv_sem=rrecv.at[c, i],
            device_id=(me, target),
            device_id_type=MESH,
        )

    def give_back(k):
        return pltpu.make_async_remote_copy(
            src_ref=outbox.at[lax.div(k, PER), block(lax.rem(k, PER))],
            dst_ref=back.at[block(k)],
            send_sem=bsend.at[k],
            recv_sem=brecv.at[k],
            device_id=(behind(k), x),
            device_id_type=MESH,
        )

    own_out = pltpu.make_async_copy(
        outbox.at[0, pl.ds(0, MAIN)], back.at[pl.ds(0, MAIN)], local_sem.at[1]
    )

    def project(act, quarter):
        columns = pl.ds(pl.multiple_of(quarter * cols, cols), cols)
        return jnp.dot(act, down[:, columns], preferred_element_type=jnp.float32)

    def compute(c):
        tails = jnp.concatenate([inbox[c, m, :, cols:] for m in range(4)], axis=1)
        tails = jnp.dot(sort[...], tails, preferred_element_type=jnp.float32).astype(jnp.bfloat16)
        for m in range(4):
            extra = jnp.concatenate(
                [
                    tails[g * CHUNK_OVER : (g + 1) * CHUNK_OVER, m * LANES : (m + 1) * LANES]
                    for g in range(groups)
                ],
                axis=1,
            )
            rows = jnp.concatenate([inbox[c, m, :, :cols], extra], axis=0)
            part = jnp.dot(
                rows, gate_up[m * cols : (m + 1) * cols, :], preferred_element_type=jnp.float32
            )
            if m == 0:
                acc[...] = part
            else:
                acc[...] += part
        gate, up = acc[:, :ff], acc[:, ff:]
        act = (gate / (1.0 + jnp.exp(-gate)) * up).astype(jnp.bfloat16)
        to_far[c] = project(act, far).astype(jnp.bfloat16)
        reduce(c, 0).start()
        reduce(c, 1).start()
        to_right[c] = project(act, right).astype(jnp.bfloat16)
        to_left[c] = project(act, left).astype(jnp.bfloat16)
        own[c] = project(act, x)

    @pl.loop(0, CHUNKS + 4)
    def _(t):
        @pl.when(t < CHUNKS)
        def _():
            @pl.loop(0, PER)
            def _(j):
                @pl.when(t * PER + j > 0)
                def _():
                    dispatch(t * PER + j).wait_recv()

            for i in (0, 2, 1, 3):
                gather(t, i).start()

        @pl.when((t >= 1) & (t < CHUNKS + 1))
        def _():
            c = t - 1
            gather(c, 0).wait_recv()
            gather(c, 4).start()
            gather(c, 2).wait_recv()
            gather(c, 5).start()

        @pl.when(t == 2)
        def _():
            for copy in weights:
                copy.wait()

        @pl.when((t >= 2) & (t < CHUNKS + 2))
        def _():
            c = t - 2
            for i in (1, 3, 4, 5):
                gather(c, i).wait_recv()
            compute(c)

        @pl.when((t >= 3) & (t < CHUNKS + 3))
        def _():
            c = t - 3
            reduce(c, 0).wait_recv()
            to_right[c, :HALF_OUT] = (
                to_right[c, :HALF_OUT].astype(jnp.float32) + far_a[c].astype(jnp.float32)
            ).astype(jnp.bfloat16)
            reduce(c, 2).start()
            reduce(c, 1).wait_recv()
            to_left[c, HALF_OUT:] = (
                to_left[c, HALF_OUT:].astype(jnp.float32) + far_b[c].astype(jnp.float32)
            ).astype(jnp.bfloat16)
            reduce(c, 3).start()

        @pl.when(t >= 4)
        def _():
            c = t - 4
            reduce(c, 2).wait_recv()
            reduce(c, 3).wait_recv()
            total = (
                own[c] + from_left[c].astype(jnp.float32) + from_right[c].astype(jnp.float32)
            ).astype(jnp.bfloat16)
            outbox[c, :, :cols] = total[:CHUNK_MAIN]
            extra = jnp.concatenate(
                [total[CHUNK_MAIN:, g * LANES : (g + 1) * LANES] for g in range(groups)], axis=0
            )
            outbox[c, :, cols:] = jnp.dot(
                unsort[...], extra, preferred_element_type=jnp.float32
            ).astype(jnp.bfloat16)

            @pl.when(c == 0)
            def _():
                own_out.start()

            @pl.loop(0, PER)
            def _(j):
                @pl.when(c * PER + j > 0)
                def _():
                    give_back(c * PER + j).start()

    own_out.wait()

    @pl.loop(1, EXPERTS)
    def _(k):
        give_back(k).wait_recv()

    @pl.loop(1, EXPERTS)
    def _(k):
        dispatch(k).wait_send()
        give_back(k).wait_send()

    @pl.loop(0, CHUNKS)
    def _(c):
        for i in range(6):
            gather(c, i).wait_send()
        for i in range(4):
            reduce(c, i).wait_send()


def experts(packed, w_gate, w_up, w_down):
    width = packed.shape[1]
    cols = width - LANES
    ff, model_width = w_down.shape
    order = overflow_order()
    rows = CHUNK_ROWS
    bf16, f32 = jnp.bfloat16, jnp.float32
    dma = pltpu.SemaphoreType.DMA
    anywhere = pl.BlockSpec(memory_space=pl.ANY)
    onchip = pl.BlockSpec(memory_space=pltpu.VMEM)
    return pl.pallas_call(
        expert_kernel,
        out_shape=jax.ShapeDtypeStruct(packed.shape, bf16),
        in_specs=[anywhere] * 4 + [onchip] * 2,
        out_specs=anywhere,
        scratch_shapes=[
            pltpu.VMEM((CHUNKS, 4, CHUNK_MAIN, width), bf16),
            pltpu.VMEM((model_width, 2 * ff), bf16),
            pltpu.VMEM((ff, model_width), bf16),
            pltpu.VMEM((rows, 2 * ff), f32),
            pltpu.VMEM((CHUNKS, rows, cols), bf16),
            pltpu.VMEM((CHUNKS, rows, cols), bf16),
            pltpu.VMEM((CHUNKS, rows, cols), bf16),
            pltpu.VMEM((CHUNKS, rows, cols), f32),
            pltpu.VMEM((CHUNKS, HALF_OUT, cols), bf16),
            pltpu.VMEM((CHUNKS, rows - HALF_OUT, cols), bf16),
            pltpu.VMEM((CHUNKS, rows, cols), bf16),
            pltpu.VMEM((CHUNKS, rows, cols), bf16),
            pltpu.VMEM((CHUNKS, CHUNK_MAIN, width), bf16),
            dma((3,)),
            dma((2,)),
            dma((EXPERTS,)),
            dma((EXPERTS,)),
            dma((CHUNKS, 6)),
            dma((CHUNKS, 6)),
            dma((CHUNKS, 4)),
            dma((CHUNKS, 4)),
            dma((EXPERTS,)),
            dma((EXPERTS,)),
        ],
        compiler_params=pltpu.CompilerParams(
            collective_id=1, has_side_effects=True, vmem_limit_bytes=58 << 20
        ),
    )(packed, w_gate, w_up, w_down, jnp.asarray(order, bf16), jnp.asarray(order.T, bf16))


def per_device(
    attn_heads, out_proj, residual, norm_gain, route_ids, route_weights, w_gate, w_up, w_down
):
    tokens, model_width = residual.shape
    members = lax.axis_size("tensor")
    place = lax.axis_index("expert")
    cols = model_width // members
    groups = cols // LANES
    rows = EXPERTS * MAIN

    relative = ((route_ids // RING - place // RING) % ROWS_Y) * RING + (
        route_ids % RING - place % RING
    ) % RING
    rank, weight = routing(relative, route_weights)
    row = jnp.arange(rows, dtype=jnp.int32)
    slot = row % MAIN
    spread = jnp.repeat(rank, MAIN, axis=1)
    main_hit = spread == slot[None, :]
    over_hit = spread == (MAIN + slot // groups)[None, :]
    row_weight = jnp.repeat(weight, MAIN, axis=1)

    hidden, normed = attention(attn_heads, out_proj, residual, norm_gain)

    main = jnp.einsum(
        "tr,td->rd", main_hit.astype(jnp.bfloat16), normed, preferred_element_type=jnp.float32
    ).astype(jnp.bfloat16)
    wide = jnp.einsum(
        "tr,td->rd", over_hit.astype(jnp.bfloat16), normed, preferred_element_type=jnp.float32
    ).astype(jnp.bfloat16)
    own_group = (row % groups)[:, None]
    over = jnp.zeros((rows, LANES), jnp.bfloat16)
    for g in range(groups):
        over = jnp.where(own_group == g, wide[:, g * LANES : (g + 1) * LANES], over)
    packed = jnp.concatenate([main, over], axis=1)
    returned = experts(packed, w_gate[0], w_up[0], w_down[0])
    high = row_weight.astype(jnp.bfloat16)
    low = (row_weight - high.astype(jnp.float32)).astype(jnp.bfloat16)
    mixture = 0.0
    zero = jnp.zeros((), jnp.bfloat16)
    for part in (high, low):
        pick = jnp.where(main_hit, part, zero)
        mixture += jnp.dot(pick, returned[:, :cols], preferred_element_type=jnp.float32)
        extra = [
            jnp.dot(
                jnp.where(over_hit & (row % groups == g)[None, :], part, zero),
                returned[:, cols:],
                preferred_element_type=jnp.float32,
            )
            for g in range(groups)
        ]
        mixture += jnp.concatenate(extra, axis=1)
    return (hidden + mixture).astype(jnp.bfloat16)


def solution(mesh):
    placed = (
        P("expert", "tensor"),
        P("tensor", "expert"),
        P("expert", None),
        P(),
        P("expert", None),
        P("expert", None),
        P("expert", None, "tensor"),
        P("expert", None, "tensor"),
        P("expert", "tensor", None),
    )
    return jax.shard_map(
        per_device, mesh=mesh, in_specs=placed, out_specs=P("expert", "tensor"), check_vma=False
    )
```

```python
import jax
import jax.numpy as jnp
import numpy as np
from jax import lax
from jax.experimental import pallas as pl
from jax.experimental.pallas import tpu as pltpu
from jax.sharding import PartitionSpec as P

MESH = pl.DeviceIdType.MESH
EXPERTS = 64
RING = 16
ROWS_Y = EXPERTS // RING
MAIN = 16
OVER = 2
LANES = 128
GROUPS = 8
SPLIT = 768
DEPTH = 8
PER = 8
CHUNK_MAIN = PER * MAIN
CHUNK_OVER = PER * OVER
CHUNK_ROWS = CHUNK_MAIN + CHUNK_OVER
HALF_IN = CHUNK_MAIN // 2
HALF_OUT = CHUNK_ROWS // 2 // 16 * 16


def routing(ids, route_weights):
    count = ids.shape[0]
    hits = (ids[:, :, None] == jnp.arange(EXPERTS, dtype=jnp.int32)[None, None, :]).astype(
        jnp.float32
    )
    chosen = jnp.sum(hits, axis=1)
    weights = route_weights / jnp.sum(route_weights, axis=-1, keepdims=True)
    weight = jnp.sum(hits * weights[:, :, None], axis=1)
    order = jnp.arange(count, dtype=jnp.int32)
    earlier = (order[None, :] < order[:, None]).astype(jnp.bfloat16)
    rank = jnp.dot(earlier, chosen.astype(jnp.bfloat16), preferred_element_type=jnp.float32)
    rank = jnp.where(chosen > 0, rank, -1.0)
    return rank.astype(jnp.int32), weight


def overflow_order():
    groups = GROUPS
    matrix = np.zeros((CHUNK_MAIN, CHUNK_MAIN), np.float32)
    for g in range(groups):
        for s in range(PER):
            for c in range(OVER):
                matrix[g * CHUNK_OVER + s * OVER + c, s * MAIN + c * groups + g] = 1.0
    return matrix


def attention_kernel(
    heads_hbm, proj_hbm, residual_hbm, gain_hbm, hidden_out, normed_out,
    shard, sibling_shard, weight, heads, to_far, to_right, to_left, own,
    far_a, far_b, from_left, from_right, mine, arrived, residual, gain, squares,
    shared, shared_residual, shared_gain,
    local_sem, shard_sem, zsend, zrecv, csend, crecv, hsend, hrecv, rsend, rrecv, wsem, nsend, nrecv,
    ssend, srecv,
):
    me = lax.axis_index("expert")
    x = lax.axis_index("tensor")
    y, zc = lax.div(me, RING), lax.rem(me, RING)
    core, z = lax.rem(zc, 2), lax.div(zc, 2)
    depth = RING // 2
    right, left, far = lax.rem(x + 1, 4), lax.rem(x + 3, 4), lax.rem(x + 2, 4)
    sibling = me + 1 - 2 * core
    cols = weight.shape[1]
    half = weight.shape[0] // 2
    tokens = heads.shape[1]

    def along_z(step):
        return y * RING + lax.rem(z + depth + step, depth) * 2 + core

    def along_y(step):
        return lax.rem(y + step, ROWS_Y) * RING + zc

    partner = (x * RING + zc, y)
    local = [
        pltpu.make_async_copy(proj_hbm, shard, local_sem.at[0]),
        pltpu.make_async_copy(heads_hbm, heads.at[y], local_sem.at[1]),
        pltpu.make_async_copy(
            residual_hbm.at[:, pl.ds(pl.multiple_of(x * cols, cols), cols)], residual, local_sem.at[2]
        ),
        pltpu.make_async_copy(
            gain_hbm.at[:, pl.ds(pl.multiple_of(x * cols, cols), cols)], gain, local_sem.at[3]
        ),
    ]
    share = cols - SPLIT
    for m in range(4):
        local.append(
            pltpu.make_async_copy(
                residual_hbm.at[:, pl.ds(m * cols + SPLIT, share)],
                shared_residual.at[:, pl.ds(m * share, share)],
                local_sem.at[4 + m],
            )
        )
        local.append(
            pltpu.make_async_copy(
                gain_hbm.at[:, pl.ds(m * cols + SPLIT, share)],
                shared_gain.at[:, pl.ds(m * share, share)],
                local_sem.at[8 + m],
            )
        )
    for copy in local:
        copy.start()

    barrier = pltpu.get_barrier_semaphore()
    for device in (sibling, along_z(1), along_z(-1), along_y(1), along_y(2), along_y(3)):
        pl.semaphore_signal(barrier, inc=1, device_id=(device, x), device_id_type=MESH)
    for m in (right, left, far):
        pl.semaphore_signal(barrier, inc=1, device_id=(me, m), device_id_type=MESH)

    @pl.when(x != y)
    def _():
        pl.semaphore_signal(barrier, inc=1, device_id=partner, device_id_type=MESH)
        pl.semaphore_wait(barrier, 10)

    @pl.when(x == y)
    def _():
        pl.semaphore_wait(barrier, 9)

    def remote(source, landing, send, recv, device):
        return pltpu.make_async_remote_copy(
            src_ref=source,
            dst_ref=landing,
            send_sem=send,
            recv_sem=recv,
            device_id=device,
            device_id_type=MESH,
        )

    swap_shard = remote(
        shard.at[pl.ds(pl.multiple_of((1 - core) * half, half), half)],
        sibling_shard,
        shard_sem.at[0],
        shard_sem.at[1],
        (sibling, x),
    )
    local[0].wait()
    swap_shard.start()
    local[1].wait()

    def share_heads(i):
        return remote(heads.at[y], heads.at[y], hsend.at[i], hrecv.at[i], (along_y(i + 1), x))

    for i in (1, 0, 2):
        share_heads(i).start()

    def piece(owner, part):
        start = core * half + (half // 2 if part == 2 else 0)
        count = half if part == 0 else half // 2
        return weight.at[
            pl.ds(pl.multiple_of(start, half // 2), count),
            pl.ds(pl.multiple_of(owner * LANES, LANES), LANES),
        ]

    def ring(direction, s):
        offset = -(s - 1) if direction == 0 else s - 1
        ref = piece(
            lax.rem(z + depth + offset, depth), (1 + direction) if s == depth // 2 else 0
        )
        target = along_z(1 if direction == 0 else -1)
        return remote(ref, ref, zsend.at[direction, s - 1], zrecv.at[direction, s - 1], (target, x))

    def across(direction, s):
        offset = -s if direction == 0 else s
        ref = piece(
            lax.rem(z + depth + offset, depth), (1 + direction) if s == depth // 2 else 0
        )
        i = 5 * direction + s
        return remote(ref, ref, csend.at[i], crecv.at[i], (sibling, x))

    width = shard.shape[1]
    row = lax.broadcasted_iota(jnp.int32, (width, LANES), 0)
    lane = lax.broadcasted_iota(jnp.int32, (width, LANES), 1)
    put_own = (lane == row + width * core).astype(jnp.bfloat16)
    put_other = (lane == row + width * (1 - core)).astype(jnp.bfloat16)
    swap_shard.wait_recv()
    both = jnp.dot(
        shard[pl.ds(pl.multiple_of(core * half, half), half), :],
        put_own,
        preferred_element_type=jnp.float32,
    ) + jnp.dot(sibling_shard[...], put_other, preferred_element_type=jnp.float32)
    weight[
        pl.ds(pl.multiple_of(core * half, half), half),
        pl.ds(pl.multiple_of(z * LANES, LANES), LANES),
    ] = both.astype(jnp.bfloat16)
    ring(0, 1).start()
    ring(1, 1).start()
    across(0, 0).start()
    for s in range(1, depth // 2 + 1):
        for direction in (0, 1):
            ring(direction, s).wait_recv()
            if s < depth // 2:
                ring(direction, s + 1).start()
            across(direction, s).start()
    handed = [(0, 0)] + [(d, s) for s in range(1, depth // 2 + 1) for d in (0, 1)]
    for i in (0, 2, 1):
        share_heads(i).wait_recv()
    for d, s in handed:
        across(d, s).wait_recv()

    def partial(block):
        return jnp.dot(heads[block], weight[...], preferred_element_type=jnp.float32)

    part = tokens // 2

    def reduce(i):
        source = (to_far.at[pl.ds(0, part)], to_far.at[pl.ds(part, part)], to_right, to_left)[i]
        landing = (far_a, far_b, from_left, from_right)[i]
        target = (right, left, right, left)[i]
        return remote(source, landing, rsend.at[i], rrecv.at[i], (me, target))

    to_far[...] = partial(far).astype(jnp.bfloat16)
    reduce(0).start()
    reduce(1).start()
    via_right = partial(right)
    reduce(0).wait_recv()
    to_right[:part] = (via_right[:part] + far_a[...].astype(jnp.float32)).astype(jnp.bfloat16)
    to_right[part:] = via_right[part:].astype(jnp.bfloat16)
    reduce(2).start()
    via_left = partial(left)
    reduce(1).wait_recv()
    to_left[:part] = via_left[:part].astype(jnp.bfloat16)
    to_left[part:] = (via_left[part:] + far_b[...].astype(jnp.float32)).astype(jnp.bfloat16)
    reduce(3).start()
    own[...] = partial(x)
    reduce(2).wait_recv()
    reduce(3).wait_recv()
    mine[...] = (
        own[...] + from_left[...].astype(jnp.float32) + from_right[...].astype(jnp.float32)
    ).astype(jnp.bfloat16)
    exchange = remote(mine, arrived, wsem.at[0], wsem.at[1], partner)

    @pl.when(x != y)
    def _():
        exchange.start()
        exchange.wait_recv()
        exchange.wait_send()

    @pl.when(x == y)
    def _():
        arrived[...] = mine[...]

    shared[x] = arrived[:, SPLIT:]

    def share_features(i):
        return remote(
            shared.at[x], shared.at[x], ssend.at[i], srecv.at[i], (me, (right, far, left)[i])
        )

    for i in range(3):
        share_features(i).start()
    for copy in local[2:]:
        copy.wait()
    hidden = residual[...].astype(jnp.float32) + arrived[...].astype(jnp.float32)
    hidden_out[...] = hidden
    squares[0] = jnp.broadcast_to(
        jnp.sum(hidden * hidden, axis=-1, keepdims=True), (tokens, LANES)
    )

    def share_squares(i):
        return remote(
            squares.at[0], squares.at[i + 1], nsend.at[i], nrecv.at[i], (me, (right, far, left)[i])
        )

    for i in range(3):
        share_squares(i).start()
    for i in range(3):
        share_squares(i).wait_recv()
        share_features(i).wait_recv()
    mean = (squares[0] + squares[1] + squares[2] + squares[3]) / (4 * cols)
    scale = lax.rsqrt(mean + 1e-06)[:, :1]
    normed_out[:, :SPLIT] = (hidden[:, :SPLIT] * scale * gain[:, :SPLIT]).astype(jnp.bfloat16)
    for m in range(4):
        lanes = slice(m * share, (m + 1) * share)
        value = shared_residual[:, lanes].astype(jnp.float32) + shared[m].astype(jnp.float32)
        normed_out[:, SPLIT + m * share : SPLIT + (m + 1) * share] = (
            value * scale * shared_gain[:, lanes]
        ).astype(jnp.bfloat16)

    swap_shard.wait_send()
    for i in range(3):
        share_heads(i).wait_send()
        share_squares(i).wait_send()
        share_features(i).wait_send()
    for d, s in handed:
        across(d, s).wait_send()
    for s in range(1, depth // 2 + 1):
        for direction in (0, 1):
            ring(direction, s).wait_send()
    for i in range(4):
        reduce(i).wait_send()


def attention(attn_heads, out_proj, residual, norm_gain):
    tokens, depth = attn_heads.shape
    cols = residual.shape[1] // 4
    bf16, f32 = jnp.bfloat16, jnp.float32
    dma = pltpu.SemaphoreType.DMA
    anywhere = pl.BlockSpec(memory_space=pl.ANY)
    onchip = pl.BlockSpec(memory_space=pltpu.VMEM)
    block = pltpu.VMEM((tokens, cols), bf16)
    return pl.pallas_call(
        attention_kernel,
        out_shape=(
            jax.ShapeDtypeStruct((tokens, cols), f32),
            jax.ShapeDtypeStruct((tokens, SPLIT + 4 * (cols - SPLIT)), bf16),
        ),
        in_specs=[anywhere] * 4,
        out_specs=(onchip, onchip),
        scratch_shapes=[
            pltpu.VMEM(out_proj.shape, bf16),
            pltpu.VMEM((depth // 2, out_proj.shape[1]), bf16),
            pltpu.VMEM((depth, cols), bf16),
            pltpu.VMEM((ROWS_Y, tokens, depth), bf16),
            block,
            block,
            block,
            pltpu.VMEM((tokens, cols), f32),
            pltpu.VMEM((tokens // 2, cols), bf16),
            pltpu.VMEM((tokens // 2, cols), bf16),
            block,
            block,
            block,
            block,
            block,
            pltpu.VMEM((1, cols), f32),
            pltpu.VMEM((4, tokens, LANES), f32),
            pltpu.VMEM((4, tokens, cols - SPLIT), bf16),
            pltpu.VMEM((tokens, 4 * (cols - SPLIT)), bf16),
            pltpu.VMEM((1, 4 * (cols - SPLIT)), f32),
            dma((12,)),
            dma((2,)),
            dma((2, 4)),
            dma((2, 4)),
            dma((10,)),
            dma((10,)),
            dma((3,)),
            dma((3,)),
            dma((4,)),
            dma((4,)),
            dma((2,)),
            dma((3,)),
            dma((3,)),
            dma((3,)),
            dma((3,)),
        ],
        compiler_params=pltpu.CompilerParams(
            collective_id=2, has_side_effects=True, vmem_limit_bytes=32 << 20
        ),
    )(attn_heads, out_proj, residual, norm_gain[None, :])


def expert_kernel(
    normed, routes_in, hidden, gate_hbm, up_hbm, down_hbm, sort, unsort, out,
    tokens_in, routes, packed, inbox, inner, gate_up, down, acc,
    to_far, to_right, to_left, own, far_a, far_b, from_left, from_right,
    returned, planes, total, staged, quarters,
    local_sem, zsend, zrecv, tsend, trecv, ysend, yrecv, asend, arecv,
    rsend, rrecv, bsend, brecv, msend, mrecv, fsend, frecv,
):
    me = lax.axis_index("expert")
    x = lax.axis_index("tensor")
    y, zc = lax.div(me, RING), lax.rem(me, RING)
    core, z = lax.rem(zc, 2), lax.div(zc, 2)
    right, left, far = lax.rem(x + 1, 4), lax.rem(x + 3, 4), lax.rem(x + 2, 4)
    ff = gate_hbm.shape[1]
    cols = hidden.shape[1]
    share = cols - SPLIT
    inner_width = SPLIT + LANES
    first = inner_width
    last = first + 4 * share
    bf16, f32 = jnp.bfloat16, jnp.float32

    def along_z(step):
        return y * RING + lax.rem(z + DEPTH + step, DEPTH) * 2 + core

    def distance(i):
        odd = lax.rem(i, 2)
        return lax.rem(odd * lax.div(i + 1, 2) + (1 - odd) * (DEPTH - lax.div(i, 2)), DEPTH)

    def plane(dy, dc):
        return lax.rem(y + ROWS_Y + dy, ROWS_Y) * RING + z * 2 + lax.rem(core + dc, 2)

    def remote(source, landing, send, recv, device):
        return pltpu.make_async_remote_copy(
            src_ref=source,
            dst_ref=landing,
            send_sem=send,
            recv_sem=recv,
            device_id=device,
            device_id_type=MESH,
        )

    weights = [
        pltpu.make_async_copy(gate_hbm, gate_up.at[:, pl.ds(0, ff)], local_sem.at[0]),
        pltpu.make_async_copy(up_hbm, gate_up.at[:, pl.ds(ff, ff)], local_sem.at[1]),
        pltpu.make_async_copy(down_hbm, down, local_sem.at[2]),
    ]
    load_tokens = pltpu.make_async_copy(normed, tokens_in.at[0], local_sem.at[3])
    load_routes = pltpu.make_async_copy(routes_in.at[0], routes.at[0], local_sem.at[4])
    load_tokens.start()
    load_routes.start()
    for copy in weights:
        copy.start()

    barrier = pltpu.get_barrier_semaphore()

    @pl.loop(1, DEPTH)
    def _(i):
        pl.semaphore_signal(barrier, inc=1, device_id=(along_z(i), x), device_id_type=MESH)
        pl.semaphore_signal(
            barrier,
            inc=1,
            device_id=(plane(lax.div(i, 2), lax.rem(i, 2)), x),
            device_id_type=MESH,
        )

    for m in (right, far, left):
        pl.semaphore_signal(barrier, inc=1, device_id=(me, m), device_id_type=MESH)
    pl.semaphore_wait(barrier, 2 * (DEPTH - 1) + 3)

    def block(k):
        return pl.ds(pl.multiple_of(k * MAIN, MAIN), MAIN)

    def send_routes(i):
        return remote(
            routes_in.at[i], routes.at[i], tsend.at[i], trecv.at[i], (along_z(distance(i)), x)
        )

    def ring(i, before=None):
        before = lax.rem(i + DEPTH - 2, DEPTH) if before is None else before
        return remote(
            tokens_in.at[before],
            tokens_in.at[i],
            zsend.at[i],
            zrecv.at[i],
            (along_z(2 * lax.rem(i, 2) - 1), x),
        )

    middle = tokens_in.shape[1] // 2

    def ring_far(side):
        rows = pl.ds(side * middle, middle)
        return remote(
            tokens_in.at[DEPTH - 3 + side, rows],
            tokens_in.at[DEPTH - 1, rows],
            zsend.at[DEPTH - 1 + side],
            zrecv.at[DEPTH - 1 + side],
            (along_z(1 - 2 * side), x),
        )

    load_tokens.wait()
    ring(1, 0).start()
    ring(2, 0).start()

    @pl.loop(1, DEPTH)
    def _(i):
        send_routes(i).start()

    load_routes.wait()

    def exchange(i, k):
        return remote(
            packed.at[i, block(k)],
            inbox.at[i, block(k)],
            ysend.at[i, k],
            yrecv.at[i, k],
            (plane(lax.div(k, 2), lax.rem(k, 2)), x),
        )

    def give_back(i, k):
        return remote(
            packed.at[i, block(k)],
            returned.at[i, block(k)],
            bsend.at[i, k],
            brecv.at[i, k],
            (plane(-lax.div(k, 2), lax.rem(k, 2)), x),
        )

    low, high = pl.ds(0, HALF_IN), pl.ds(HALF_IN, HALF_IN)

    def gather(c, i):
        owner = (x, x, x, x, left, right)[i]
        part = (low, high, high, low, low, high)[i]
        target = (right, right, left, left, right, left)[i]
        ref = inner.at[c, owner, part]
        return remote(ref, ref, asend.at[c, i], arecv.at[c, i], (me, target))

    head, tail = pl.ds(0, HALF_OUT), pl.ds(HALF_OUT, CHUNK_ROWS - HALF_OUT)

    def reduce(c, i):
        source = (to_far.at[c, head], to_far.at[c, tail], to_right.at[c], to_left.at[c])[i]
        landing = (far_a.at[c], far_b.at[c], from_left.at[c], from_right.at[c])[i]
        return remote(
            source, landing, rsend.at[c, i], rrecv.at[c, i], (me, (right, left, right, left)[i])
        )

    def send_plane(i):
        return remote(
            tokens_in.at[i], planes.at[i], msend.at[i], mrecv.at[i], (along_z(-distance(i)), x)
        )

    def send_quarter(i):
        m = (right, far, left)[i]
        return remote(
            staged.at[:, pl.ds(pl.multiple_of(m * share, share), share)],
            quarters.at[i],
            fsend.at[i],
            frecv.at[i],
            (me, m),
        )

    square = (CHUNK_MAIN, CHUNK_MAIN)
    row = lax.broadcasted_iota(jnp.int32, square, 0)
    row_slot = (row & (MAIN - 1)).astype(f32)
    row_over = (MAIN + ((row & (MAIN - 1)) >> 3)).astype(f32)
    row_group = row & (GROUPS - 1)
    lane_group = lax.broadcasted_iota(jnp.int32, square, 1) & (GROUPS - 1)

    def spread(values):
        return jnp.broadcast_to(values[:, None, :], (PER, MAIN, LANES)).reshape(square)

    def dot(a, b):
        return jnp.dot(a, b, preferred_element_type=f32)

    def pick(i):
        rank = spread(routes[i, :PER])
        tokens = tokens_in[i]
        chosen = dot(jnp.where(rank == row_slot, 1.0, 0.0).astype(bf16), tokens)
        packed[i, :, :SPLIT] = chosen[:, :SPLIT].astype(bf16)
        packed[i, :, first:last] = chosen[:, SPLIT:].astype(bf16)
        wide = dot(jnp.where(rank == row_over, 1.0, 0.0).astype(bf16), tokens)
        for start, count, lane in ((0, SPLIT // LANES, SPLIT), (SPLIT, GROUPS, last)):
            tile = jnp.zeros(square, f32)
            for g in range(count):
                piece = wide[:, start + g * LANES : start + (g + 1) * LANES]
                tile = jnp.where(row_group == g, piece, tile)
            packed[i, :, lane : lane + LANES] = tile.astype(bf16)
        inbox[i, :MAIN] = packed[i, :MAIN]

        @pl.loop(1, PER)
        def _(k):
            exchange(i, k).start()

    def project(act, quarter):
        columns = pl.ds(pl.multiple_of(quarter * cols, cols), cols)
        return dot(act, down[:, columns])

    def compute(c):
        @pl.loop(1, PER)
        def _(k):
            exchange(c, k).wait_send()

        tails = jnp.concatenate(
            [inner[c, m, :, SPLIT:] for m in range(4)] + [inbox[c, :, last:]], axis=1
        )
        tails = dot(sort[...], tails).astype(bf16)

        def tail_piece(g, tile):
            return tails[g * CHUNK_OVER : (g + 1) * CHUNK_OVER, tile * LANES : (tile + 1) * LANES]

        per_share = share // LANES
        for m in range(4):
            extra = [tail_piece(g, m) for g in range(SPLIT // LANES)] + [
                tail_piece(m * per_share + g, 4) for g in range(per_share)
            ]
            body = jnp.concatenate(
                [
                    inner[c, m, :, :SPLIT],
                    inbox[c, :, first + m * share : first + (m + 1) * share],
                ],
                axis=1,
            )
            rows = jnp.concatenate([body, jnp.concatenate(extra, axis=1)], axis=0)
            part = dot(rows, gate_up[m * cols : (m + 1) * cols, :])
            if m == 0:
                acc[...] = part
            else:
                acc[...] += part
        gate, up = acc[:, :ff], acc[:, ff:]
        act = (gate / (1.0 + jnp.exp(-gate)) * up).astype(bf16)

        def keep_share(quarter, value):
            lanes = pl.ds(pl.multiple_of(first + quarter * share, LANES), share)
            packed[c, :, lanes] = value[:CHUNK_MAIN, SPLIT:].astype(bf16)
            staging = pl.ds(pl.multiple_of(quarter * share, share), share)
            staged[:CHUNK_OVER, staging] = value[CHUNK_MAIN:, SPLIT:].astype(bf16)

        value = project(act, far)
        to_far[c] = value[:, :SPLIT].astype(bf16)
        reduce(c, 0).start()
        reduce(c, 1).start()
        keep_share(far, value)
        value = project(act, right)
        to_right[c] = value[:, :SPLIT].astype(bf16)
        keep_share(right, value)
        value = project(act, left)
        to_left[c] = value[:, :SPLIT].astype(bf16)
        keep_share(left, value)
        value = project(act, x)
        own[c] = value[:, :SPLIT]
        keep_share(x, value)
        over = staged[:CHUNK_OVER, :]
        over = jnp.concatenate(
            [over[:, g * LANES : (g + 1) * LANES] for g in range(GROUPS)], axis=0
        )
        packed[c, :, last:] = dot(unsort[...], over).astype(bf16)

    def finish(c):
        reduce(c, 2).wait_recv()
        reduce(c, 3).wait_recv()
        value = (
            own[c] + from_left[c].astype(f32) + from_right[c].astype(f32)
        ).astype(bf16)
        packed[c, :, :SPLIT] = value[:CHUNK_MAIN]
        count = SPLIT // LANES
        over = jnp.concatenate(
            [value[CHUNK_MAIN:, g * LANES : (g + 1) * LANES] for g in range(count)]
            + [jnp.zeros(((GROUPS - count) * CHUNK_OVER, LANES), bf16)],
            axis=0,
        )
        packed[c, :, SPLIT:first] = dot(unsort[...], over).astype(bf16)
        returned[c, :MAIN] = packed[c, :MAIN]

        @pl.loop(1, PER)
        def _(k):
            give_back(c, k).start()

    def combine(c):
        @pl.loop(1, PER)
        def _(k):
            give_back(c, k).wait_recv()

        rank, weight = spread(routes[c, :PER]), spread(routes[c, PER:])
        rows = returned[c]
        whole = jnp.where(rank == row_slot, weight, 0.0).T
        over = jnp.where(rank == row_over, weight, 0.0).T
        high_part = whole.astype(bf16)
        low_part = (whole - high_part.astype(f32)).astype(bf16)
        mixed = dot(high_part, rows) + dot(low_part, rows)
        tiles = jnp.concatenate([rows[:, SPLIT:first], rows[:, last:]], axis=1)
        extra = []
        for g in range(GROUPS):
            picked = jnp.where(lane_group == g, over, 0.0)
            high_part = picked.astype(bf16)
            low_part = (picked - high_part.astype(f32)).astype(bf16)
            extra.append(dot(high_part, tiles) + dot(low_part, tiles))
        count = SPLIT // LANES
        inner_sum = mixed[:, :SPLIT] + jnp.concatenate(
            [extra[g][:, :LANES] for g in range(count)], axis=1
        )
        share_sum = mixed[:, first:last] + jnp.concatenate(
            [extra[g][:, LANES:] for g in range(GROUPS)], axis=1
        )

        @pl.when(c == 0)
        def _():
            total[:, :SPLIT] = inner_sum
            total[:, SPLIT:] = share_sum

        @pl.when((c >= 1) & (c <= DEPTH - 4))
        def _():
            ring(c + 2).wait_send()

        for side in (0, 1):

            @pl.when(c == DEPTH - 3 + side)
            def _():
                ring_far(side).wait_send()

        @pl.when(c > 0)
        def _():
            tokens_in[c, :, :SPLIT] = inner_sum.astype(bf16)
            tokens_in[c, :, SPLIT:] = share_sum.astype(bf16)
            send_plane(c).start()

    pick(0)

    @pl.loop(0, DEPTH + 5)
    def _(t):
        @pl.when(t < DEPTH)
        def _():
            @pl.loop(1, PER)
            def _(k):
                exchange(t, k).wait_recv()

            inner[t, x] = inbox[t, :, :inner_width]
            for i in (0, 2, 1, 3):
                gather(t, i).start()

        @pl.when((t >= 1) & (t < DEPTH + 1))
        def _():
            c = t - 1
            gather(c, 0).wait_recv()
            gather(c, 4).start()
            gather(c, 2).wait_recv()
            gather(c, 5).start()

        @pl.when(t + 1 < DEPTH)
        def _():
            i = t + 1

            @pl.when(i < DEPTH - 1)
            def _():
                ring(i).wait_recv()

            @pl.when(i + 2 < DEPTH - 1)
            def _():
                ring(i + 2).start()

            for side in (0, 1):

                @pl.when(i == DEPTH - 3 + side)
                def _():
                    ring_far(side).start()

                @pl.when(i == DEPTH - 1)
                def _():
                    ring_far(side).wait_recv()

            send_routes(i).wait_recv()
            pick(i)

        @pl.when(t == 2)
        def _():
            for copy in weights:
                copy.wait()

        @pl.when((t >= 2) & (t < DEPTH + 2))
        def _():
            c = t - 2
            for i in (1, 3, 4, 5):
                gather(c, i).wait_recv()
            compute(c)

        @pl.when((t >= 3) & (t < DEPTH + 3))
        def _():
            c = t - 3
            reduce(c, 0).wait_recv()
            to_right[c, :HALF_OUT] = (
                to_right[c, :HALF_OUT].astype(f32) + far_a[c].astype(f32)
            ).astype(bf16)
            reduce(c, 2).start()
            reduce(c, 1).wait_recv()
            to_left[c, HALF_OUT:] = (
                to_left[c, HALF_OUT:].astype(f32) + far_b[c].astype(f32)
            ).astype(bf16)
            reduce(c, 3).start()

        @pl.when((t >= 4) & (t < DEPTH + 4))
        def _():
            finish(t - 4)

        @pl.when(t >= 5)
        def _():
            combine(t - 5)

    @pl.loop(1, DEPTH)
    def _(i):
        send_plane(i).wait_recv()
        total[...] += planes[i].astype(f32)

    staged[...] = total[:, SPLIT:].astype(bf16)
    for i in range(3):
        send_quarter(i).start()
    out[:, :SPLIT] = (hidden[:, :SPLIT] + total[:, :SPLIT]).astype(bf16)
    mixture = total[:, pl.ds(pl.multiple_of(SPLIT + x * share, share), share)]
    for i in range(3):
        send_quarter(i).wait_recv()
        mixture += quarters[i].astype(f32)
    out[:, SPLIT:] = (hidden[:, SPLIT:] + mixture).astype(bf16)

    for i in (1, 2):
        ring(i, 0).wait_send()
    for i in range(3):
        send_quarter(i).wait_send()

    @pl.loop(1, DEPTH)
    def _(i):
        send_routes(i).wait_send()
        send_plane(i).wait_send()

    @pl.loop(0, DEPTH)
    def _(c):
        for i in range(6):
            gather(c, i).wait_send()
        for i in range(4):
            reduce(c, i).wait_send()

        @pl.loop(1, PER)
        def _(k):
            give_back(c, k).wait_send()


def experts(normed, routes, hidden, w_gate, w_up, w_down):
    tokens, wide = normed.shape
    cols = hidden.shape[1]
    ff, model_width = w_down.shape
    order = overflow_order()
    rows = CHUNK_ROWS
    width = wide + 2 * LANES
    bf16, f32 = jnp.bfloat16, jnp.float32
    dma = pltpu.SemaphoreType.DMA
    anywhere = pl.BlockSpec(memory_space=pl.ANY)
    onchip = pl.BlockSpec(memory_space=pltpu.VMEM)
    moved = pltpu.VMEM((DEPTH, rows, SPLIT), bf16)
    return pl.pallas_call(
        expert_kernel,
        out_shape=jax.ShapeDtypeStruct((tokens, cols), bf16),
        in_specs=[anywhere] * 2 + [onchip] + [anywhere] * 3 + [onchip] * 2,
        out_specs=onchip,
        scratch_shapes=[
            pltpu.VMEM((DEPTH, tokens, wide), bf16),
            pltpu.VMEM((DEPTH, 2 * PER, LANES), f32),
            pltpu.VMEM((DEPTH, CHUNK_MAIN, width), bf16),
            pltpu.VMEM((DEPTH, CHUNK_MAIN, width), bf16),
            pltpu.VMEM((DEPTH, 4, CHUNK_MAIN, SPLIT + LANES), bf16),
            pltpu.VMEM((model_width, 2 * ff), bf16),
            pltpu.VMEM((ff, model_width), bf16),
            pltpu.VMEM((rows, 2 * ff), f32),
            moved,
            moved,
            moved,
            pltpu.VMEM((DEPTH, rows, SPLIT), f32),
            pltpu.VMEM((DEPTH, HALF_OUT, SPLIT), bf16),
            pltpu.VMEM((DEPTH, rows - HALF_OUT, SPLIT), bf16),
            moved,
            moved,
            pltpu.VMEM((DEPTH, CHUNK_MAIN, width), bf16),
            pltpu.VMEM((DEPTH, tokens, wide), bf16),
            pltpu.VMEM((tokens, wide), f32),
            pltpu.VMEM((tokens, wide - SPLIT), bf16),
            pltpu.VMEM((3, tokens, cols - SPLIT), bf16),
            dma((5,)),
            dma((DEPTH + 1,)),
            dma((DEPTH + 1,)),
            dma((DEPTH,)),
            dma((DEPTH,)),
            dma((DEPTH, PER)),
            dma((DEPTH, PER)),
            dma((DEPTH, 6)),
            dma((DEPTH, 6)),
            dma((DEPTH, 4)),
            dma((DEPTH, 4)),
            dma((DEPTH, PER)),
            dma((DEPTH, PER)),
            dma((DEPTH,)),
            dma((DEPTH,)),
            dma((3,)),
            dma((3,)),
        ],
        compiler_params=pltpu.CompilerParams(
            collective_id=1, has_side_effects=True, vmem_limit_bytes=60 << 20
        ),
    )(normed, routes, hidden, w_gate, w_up, w_down, jnp.asarray(order, bf16), jnp.asarray(order.T, bf16))


def per_device(
    attn_heads, out_proj, residual, norm_gain, route_ids, route_weights, w_gate, w_up, w_down
):
    place = lax.axis_index("expert")
    ahead_z = (route_ids % RING // 2 - place % RING // 2) % DEPTH
    chunk = jnp.where(
        ahead_z == 0, 0, jnp.where(ahead_z <= DEPTH // 2, 2 * ahead_z - 1, 2 * (DEPTH - ahead_z))
    )
    ahead_y = (route_ids // RING - place // RING) % ROWS_Y
    relative = chunk * PER + ahead_y * 2 + (route_ids - place) % 2
    rank, weight = routing(relative, route_weights)
    routes = jnp.concatenate(
        [
            rank.T.astype(jnp.float32).reshape(DEPTH, PER, -1),
            weight.T.reshape(DEPTH, PER, -1),
        ],
        axis=1,
    )
    hidden, normed = attention(attn_heads, out_proj, residual, norm_gain)
    return experts(normed, routes, hidden, w_gate[0], w_up[0], w_down[0])


def solution(mesh):
    placed = (
        P("expert", "tensor"),
        P("tensor", "expert"),
        P("expert", None),
        P(),
        P("expert", None),
        P("expert", None),
        P("expert", None, "tensor"),
        P("expert", None, "tensor"),
        P("expert", "tensor", None),
    )
    return jax.shard_map(
        per_device, mesh=mesh, in_specs=placed, out_specs=P("expert", "tensor"), check_vma=False
    )
```

```python
import jax
import jax.numpy as jnp
from jax import lax
from jax.experimental import pallas as pl
from jax.experimental.pallas import tpu as pltpu
from jax.sharding import PartitionSpec as P

MESH = pl.DeviceIdType.MESH
EXPERTS = 64
RING = 16
ROWS_Y = EXPERTS // RING
MAIN = 16
OVER = 2
LANES = 128
GROUPS = 8
SPLIT = 768
DEPTH = 8
PER = 8
CHUNK_MAIN = PER * MAIN
CHUNK_OVER = PER * OVER
CHUNK_ROWS = CHUNK_MAIN + CHUNK_OVER
HALF_IN = CHUNK_MAIN // 2
HALF_OUT = CHUNK_ROWS // 2 // 16 * 16


def attention_kernel(
    heads_hbm, proj_hbm, residual_hbm, gain_hbm, route_ids, route_weights,
    hidden_out, normed_out, routes_out,
    shard, sibling_shard, weight, heads, to_far, to_right, to_left, own,
    far_a, far_b, from_left, from_right, mine, arrived, residual, gain, squares,
    shared, shared_residual, shared_gain,
    local_sem, shard_sem, zsend, zrecv, csend, crecv, hsend, hrecv, rsend, rrecv, wsem, nsend, nrecv,
    ssend, srecv,
):
    me = lax.axis_index("expert")
    x = lax.axis_index("tensor")
    y, zc = lax.div(me, RING), lax.rem(me, RING)
    core, z = lax.rem(zc, 2), lax.div(zc, 2)
    depth = RING // 2
    right, left, far = lax.rem(x + 1, 4), lax.rem(x + 3, 4), lax.rem(x + 2, 4)
    sibling = me + 1 - 2 * core
    cols = from_left.shape[1]
    half = weight.shape[1] // 2
    tokens = heads.shape[1]

    def along_z(step):
        return y * RING + lax.rem(z + depth + step, depth) * 2 + core

    def along_y(step):
        return lax.rem(y + step, ROWS_Y) * RING + zc

    partner = (x * RING + zc, y)
    local = [
        pltpu.make_async_copy(proj_hbm, shard, local_sem.at[0]),
        pltpu.make_async_copy(heads_hbm, heads.at[y], local_sem.at[1]),
        pltpu.make_async_copy(
            residual_hbm.at[:, pl.ds(pl.multiple_of(x * cols, cols), cols)], residual, local_sem.at[2]
        ),
        pltpu.make_async_copy(
            gain_hbm.at[:, pl.ds(pl.multiple_of(x * cols, cols), cols)], gain, local_sem.at[3]
        ),
    ]
    share = cols - SPLIT
    for m in range(4):
        local.append(
            pltpu.make_async_copy(
                residual_hbm.at[:, pl.ds(m * cols + SPLIT, share)],
                shared_residual.at[:, pl.ds(m * share, share)],
                local_sem.at[4 + m],
            )
        )
        local.append(
            pltpu.make_async_copy(
                gain_hbm.at[:, pl.ds(m * cols + SPLIT, share)],
                shared_gain.at[:, pl.ds(m * share, share)],
                local_sem.at[8 + m],
            )
        )
    for copy in local:
        copy.start()

    barrier = pltpu.get_barrier_semaphore()
    for device in (sibling, along_z(1), along_z(-1), along_y(1), along_y(2), along_y(3)):
        pl.semaphore_signal(barrier, inc=1, device_id=(device, x), device_id_type=MESH)
    for m in (right, left, far):
        pl.semaphore_signal(barrier, inc=1, device_id=(me, m), device_id_type=MESH)

    @pl.when(x != y)
    def _():
        pl.semaphore_signal(barrier, inc=1, device_id=partner, device_id_type=MESH)
        pl.semaphore_wait(barrier, 10)

    @pl.when(x == y)
    def _():
        pl.semaphore_wait(barrier, 9)

    def remote(source, landing, send, recv, device):
        return pltpu.make_async_remote_copy(
            src_ref=source,
            dst_ref=landing,
            send_sem=send,
            recv_sem=recv,
            device_id=device,
            device_id_type=MESH,
        )

    swap_shard = remote(
        shard.at[pl.ds(pl.multiple_of((1 - core) * half, half), half)],
        sibling_shard,
        shard_sem.at[0],
        shard_sem.at[1],
        (sibling, x),
    )
    local[0].wait()
    swap_shard.start()
    local[1].wait()

    def share_heads(i):
        return remote(heads.at[y], heads.at[y], hsend.at[i], hrecv.at[i], (along_y(i + 1), x))

    for i in (1, 0, 2):
        share_heads(i).start()

    def piece(owner, part):
        start = core * half + (half // 2 if part == 2 else 0)
        count = half if part == 0 else half // 2
        return weight.at[owner, pl.ds(pl.multiple_of(start, half // 2), count)]

    def ring(direction, s):
        offset = -(s - 1) if direction == 0 else s - 1
        ref = piece(
            lax.rem(z + depth + offset, depth), (1 + direction) if s == depth // 2 else 0
        )
        target = along_z(1 if direction == 0 else -1)
        return remote(ref, ref, zsend.at[direction, s - 1], zrecv.at[direction, s - 1], (target, x))

    def across(direction, s):
        offset = -s if direction == 0 else s
        ref = piece(
            lax.rem(z + depth + offset, depth), (1 + direction) if s == depth // 2 else 0
        )
        i = 5 * direction + s
        return remote(ref, ref, csend.at[i], crecv.at[i], (sibling, x))

    width = shard.shape[1]
    row = lax.broadcasted_iota(jnp.int32, (width, LANES), 0)
    lane = lax.broadcasted_iota(jnp.int32, (width, LANES), 1)
    put_own = (lane == row + width * core).astype(jnp.bfloat16)
    put_other = (lane == row + width * (1 - core)).astype(jnp.bfloat16)
    swap_shard.wait_recv()
    both = jnp.dot(
        shard[pl.ds(pl.multiple_of(core * half, half), half), :],
        put_own,
        preferred_element_type=jnp.float32,
    ) + jnp.dot(sibling_shard[...], put_other, preferred_element_type=jnp.float32)
    weight[z, pl.ds(pl.multiple_of(core * half, half), half)] = both.astype(jnp.bfloat16)
    ring(0, 1).start()
    ring(1, 1).start()
    across(0, 0).start()
    square = (tokens, LANES)
    lane = lax.broadcasted_iota(jnp.int32, square, 1)
    earlier = jnp.where(lane < lax.broadcasted_iota(jnp.int32, square, 0), 1.0, 0.0)
    ids = route_ids[...]
    ahead_z = (((ids & (RING - 1)) >> 1) + depth - z) & (depth - 1)
    chunk = jnp.where(
        ahead_z == 0, 0, jnp.where(ahead_z <= depth // 2, 2 * ahead_z - 1, 2 * (depth - ahead_z))
    )
    ahead_y = ((ids >> 4) + ROWS_Y - y) & (ROWS_Y - 1)
    relative = chunk * PER + ahead_y * 2 + ((ids + 2 - core) & 1)
    shares = route_weights[...] / jnp.sum(route_weights[...], axis=-1, keepdims=True)
    chosen = jnp.zeros(square, jnp.float32)
    scaled = jnp.zeros(square, jnp.float32)
    for k in range(ids.shape[1]):
        hit = lane == relative[:, k : k + 1]
        chosen = jnp.where(hit, 1.0, chosen)
        scaled = jnp.where(hit, shares[:, k : k + 1], scaled)
    rank = jnp.dot(
        earlier.astype(jnp.bfloat16),
        chosen.astype(jnp.bfloat16),
        preferred_element_type=jnp.float32,
    )
    rank = jnp.where(chosen > 0, rank, -1.0).T
    scaled = scaled.T
    for i in range(depth):
        routes_out[i, :PER] = rank[i * PER : (i + 1) * PER]
        routes_out[i, PER:] = scaled[i * PER : (i + 1) * PER]

    for s in range(1, depth // 2 + 1):
        for direction in (0, 1):
            ring(direction, s).wait_recv()
            if s < depth // 2:
                ring(direction, s + 1).start()
            across(direction, s).start()
    handed = [(0, 0)] + [(d, s) for s in range(1, depth // 2 + 1) for d in (0, 1)]
    for i in (0, 2, 1):
        share_heads(i).wait_recv()
    for d, s in handed:
        across(d, s).wait_recv()

    def partial(block):
        return jnp.concatenate(
            [
                jnp.dot(
                    heads[block],
                    jnp.concatenate([weight[i], weight[i + 1]], axis=1),
                    preferred_element_type=jnp.float32,
                )
                for i in range(0, RING // 2, 2)
            ],
            axis=1,
        )

    part = tokens // 2

    def reduce(i):
        source = (to_far.at[pl.ds(0, part)], to_far.at[pl.ds(part, part)], to_right, to_left)[i]
        landing = (far_a, far_b, from_left, from_right)[i]
        target = (right, left, right, left)[i]
        return remote(source, landing, rsend.at[i], rrecv.at[i], (me, target))

    to_far[...] = partial(far).astype(jnp.bfloat16)
    reduce(0).start()
    reduce(1).start()
    via_right = partial(right)
    reduce(0).wait_recv()
    to_right[:part] = (via_right[:part] + far_a[...].astype(jnp.float32)).astype(jnp.bfloat16)
    to_right[part:] = via_right[part:].astype(jnp.bfloat16)
    reduce(2).start()
    via_left = partial(left)
    reduce(1).wait_recv()
    to_left[:part] = via_left[:part].astype(jnp.bfloat16)
    to_left[part:] = (via_left[part:] + far_b[...].astype(jnp.float32)).astype(jnp.bfloat16)
    reduce(3).start()
    own[...] = partial(x)
    reduce(2).wait_recv()
    reduce(3).wait_recv()
    mine[...] = (
        own[...] + from_left[...].astype(jnp.float32) + from_right[...].astype(jnp.float32)
    ).astype(jnp.bfloat16)
    exchange = remote(mine, arrived, wsem.at[0], wsem.at[1], partner)

    @pl.when(x != y)
    def _():
        exchange.start()
        exchange.wait_recv()

    @pl.when(x == y)
    def _():
        arrived[...] = mine[...]

    shared[x] = arrived[:, SPLIT:]

    def share_features(i):
        return remote(
            shared.at[x], shared.at[x], ssend.at[i], srecv.at[i], (me, (right, far, left)[i])
        )

    for i in range(3):
        share_features(i).start()
    for copy in local[2:]:
        copy.wait()
    hidden = residual[...].astype(jnp.float32) + arrived[...].astype(jnp.float32)
    hidden_out[...] = hidden
    squares[0] = jnp.broadcast_to(
        jnp.sum(hidden * hidden, axis=-1, keepdims=True), square
    ).T[:PER]

    def share_squares(i):
        return remote(
            squares.at[0], squares.at[i + 1], nsend.at[i], nrecv.at[i], (me, (right, far, left)[i])
        )

    for i in range(3):
        share_squares(i).start()
    for i in range(3):
        share_squares(i).wait_recv()
        share_features(i).wait_recv()
    mean = (squares[0] + squares[1] + squares[2] + squares[3]) / (4 * cols)
    scale = jnp.broadcast_to(lax.rsqrt(mean + 1e-06)[:1], square).T[:, :1]
    normed_out[:, :SPLIT] = (hidden[:, :SPLIT] * scale * gain[:, :SPLIT]).astype(jnp.bfloat16)
    for m in range(4):
        lanes = slice(m * share, (m + 1) * share)
        value = shared_residual[:, lanes].astype(jnp.float32) + shared[m].astype(jnp.float32)
        normed_out[:, SPLIT + m * share : SPLIT + (m + 1) * share] = (
            value * scale * shared_gain[:, lanes]
        ).astype(jnp.bfloat16)

    @pl.when(x != y)
    def _():
        exchange.wait_send()

    swap_shard.wait_send()
    for i in range(3):
        share_heads(i).wait_send()
        share_squares(i).wait_send()
        share_features(i).wait_send()
    for d, s in handed:
        across(d, s).wait_send()
    for s in range(1, depth // 2 + 1):
        for direction in (0, 1):
            ring(direction, s).wait_send()
    for i in range(4):
        reduce(i).wait_send()


def attention(attn_heads, out_proj, residual, norm_gain, route_ids, route_weights):
    tokens, depth = attn_heads.shape
    cols = residual.shape[1] // 4
    bf16, f32 = jnp.bfloat16, jnp.float32
    dma = pltpu.SemaphoreType.DMA
    anywhere = pl.BlockSpec(memory_space=pl.ANY)
    onchip = pl.BlockSpec(memory_space=pltpu.VMEM)
    block = pltpu.VMEM((tokens, cols), bf16)
    return pl.pallas_call(
        attention_kernel,
        out_shape=(
            jax.ShapeDtypeStruct((tokens, cols), f32),
            jax.ShapeDtypeStruct((tokens, SPLIT + 4 * (cols - SPLIT)), bf16),
            jax.ShapeDtypeStruct((DEPTH, 2 * PER, tokens), f32),
        ),
        in_specs=[anywhere] * 4 + [onchip] * 2,
        out_specs=(onchip, onchip, onchip),
        scratch_shapes=[
            pltpu.VMEM(out_proj.shape, bf16),
            pltpu.VMEM((depth // 2, out_proj.shape[1]), bf16),
            pltpu.VMEM((RING // 2, depth, LANES), bf16),
            pltpu.VMEM((ROWS_Y, tokens, depth), bf16),
            block,
            block,
            block,
            pltpu.VMEM((tokens, cols), f32),
            pltpu.VMEM((tokens // 2, cols), bf16),
            pltpu.VMEM((tokens // 2, cols), bf16),
            block,
            block,
            block,
            block,
            block,
            pltpu.VMEM((1, cols), f32),
            pltpu.VMEM((4, PER, LANES), f32),
            pltpu.VMEM((4, tokens, cols - SPLIT), bf16),
            pltpu.VMEM((tokens, 4 * (cols - SPLIT)), bf16),
            pltpu.VMEM((1, 4 * (cols - SPLIT)), f32),
            dma((12,)),
            dma((2,)),
            dma((2, 4)),
            dma((2, 4)),
            dma((10,)),
            dma((10,)),
            dma((3,)),
            dma((3,)),
            dma((4,)),
            dma((4,)),
            dma((2,)),
            dma((3,)),
            dma((3,)),
            dma((3,)),
            dma((3,)),
        ],
        compiler_params=pltpu.CompilerParams(
            collective_id=2, has_side_effects=True, vmem_limit_bytes=60 << 20
        ),
    )(attn_heads, out_proj, residual, norm_gain[None, :], route_ids, route_weights)


def expert_kernel(
    normed, routes_in, hidden, gate_hbm, up_hbm, down_hbm, out,
    tokens_in, routes, packed, inbox, inner, gate_up, down, acc,
    to_far, to_right, to_left, own, far_a, far_b, from_left, from_right,
    returned, planes, total, summed, staged, quarters,
    local_sem, zsend, zrecv, tsend, trecv, ysend, yrecv, asend, arecv,
    rsend, rrecv, bsend, brecv, msend, mrecv, fsend, frecv,
):
    me = lax.axis_index("expert")
    x = lax.axis_index("tensor")
    y, zc = lax.div(me, RING), lax.rem(me, RING)
    core, z = lax.rem(zc, 2), lax.div(zc, 2)
    right, left, far = lax.rem(x + 1, 4), lax.rem(x + 3, 4), lax.rem(x + 2, 4)
    ff = gate_hbm.shape[1]
    cols = hidden.shape[1]
    share = cols - SPLIT
    inner_width = SPLIT + LANES
    first = inner_width
    last = first + 4 * share
    bf16, f32 = jnp.bfloat16, jnp.float32

    def along_z(step):
        return y * RING + lax.rem(z + DEPTH + step, DEPTH) * 2 + core

    def distance(i):
        odd = lax.rem(i, 2)
        return lax.rem(odd * lax.div(i + 1, 2) + (1 - odd) * (DEPTH - lax.div(i, 2)), DEPTH)

    def plane(dy, dc):
        return lax.rem(y + ROWS_Y + dy, ROWS_Y) * RING + z * 2 + lax.rem(core + dc, 2)

    def remote(source, landing, send, recv, device):
        return pltpu.make_async_remote_copy(
            src_ref=source,
            dst_ref=landing,
            send_sem=send,
            recv_sem=recv,
            device_id=device,
            device_id_type=MESH,
        )

    weights = [
        pltpu.make_async_copy(gate_hbm, gate_up.at[:, pl.ds(0, ff)], local_sem.at[0]),
        pltpu.make_async_copy(up_hbm, gate_up.at[:, pl.ds(ff, ff)], local_sem.at[1]),
        pltpu.make_async_copy(down_hbm, down, local_sem.at[2]),
    ]
    load_tokens = pltpu.make_async_copy(normed, tokens_in.at[0], local_sem.at[3])
    load_routes = pltpu.make_async_copy(routes_in.at[0], routes.at[0], local_sem.at[4])
    load_tokens.start()
    load_routes.start()
    for copy in weights:
        copy.start()

    barrier = pltpu.get_barrier_semaphore()

    @pl.loop(1, DEPTH)
    def _(i):
        pl.semaphore_signal(barrier, inc=1, device_id=(along_z(i), x), device_id_type=MESH)
        pl.semaphore_signal(
            barrier,
            inc=1,
            device_id=(plane(lax.div(i, 2), lax.rem(i, 2)), x),
            device_id_type=MESH,
        )

    for m in (right, far, left):
        pl.semaphore_signal(barrier, inc=1, device_id=(me, m), device_id_type=MESH)
    pl.semaphore_wait(barrier, 2 * (DEPTH - 1) + 3)

    def block(k):
        return pl.ds(pl.multiple_of(k * MAIN, MAIN), MAIN)

    def send_routes(i):
        return remote(
            routes_in.at[i], routes.at[i], tsend.at[i], trecv.at[i], (along_z(distance(i)), x)
        )

    def ring(i, before=None):
        before = lax.rem(i + DEPTH - 2, DEPTH) if before is None else before
        return remote(
            tokens_in.at[before],
            tokens_in.at[i],
            zsend.at[i],
            zrecv.at[i],
            (along_z(2 * lax.rem(i, 2) - 1), x),
        )

    middle = tokens_in.shape[1] // 2

    def ring_far(side):
        rows = pl.ds(side * middle, middle)
        return remote(
            tokens_in.at[DEPTH - 3 + side, rows],
            tokens_in.at[DEPTH - 1, rows],
            zsend.at[DEPTH - 1 + side],
            zrecv.at[DEPTH - 1 + side],
            (along_z(1 - 2 * side), x),
        )

    load_tokens.wait()
    ring(1, 0).start()
    ring(2, 0).start()

    @pl.loop(1, DEPTH)
    def _(i):
        send_routes(i).start()

    load_routes.wait()

    def exchange(i, k):
        return remote(
            packed.at[i, block(k)],
            inbox.at[i, block(k)],
            ysend.at[i, k],
            yrecv.at[i, k],
            (plane(lax.div(k, 2), lax.rem(k, 2)), x),
        )

    def give_back(i, k):
        return remote(
            packed.at[i, block(k)],
            returned.at[i, block(k)],
            bsend.at[i, k],
            brecv.at[i, k],
            (plane(-lax.div(k, 2), lax.rem(k, 2)), x),
        )

    low, high = pl.ds(0, HALF_IN), pl.ds(HALF_IN, HALF_IN)

    def gather(c, i):
        owner = (x, x, x, x, left, right)[i]
        part = (low, high, high, low, low, high)[i]
        target = (right, right, left, left, right, left)[i]
        ref = inner.at[c, owner, part]
        return remote(ref, ref, asend.at[c, i], arecv.at[c, i], (me, target))

    head, tail = pl.ds(0, HALF_OUT), pl.ds(HALF_OUT, CHUNK_ROWS - HALF_OUT)

    def reduce(c, i):
        source = (to_far.at[c, head], to_far.at[c, tail], to_right.at[c], to_left.at[c])[i]
        landing = (far_a.at[c], far_b.at[c], from_left.at[c], from_right.at[c])[i]
        return remote(
            source, landing, rsend.at[c, i], rrecv.at[c, i], (me, (right, left, right, left)[i])
        )

    half_tokens = tokens_in.shape[1] // 2

    def send_plane(i):
        slot = (0, 1, 2, 3, 0, 7, 4, 5, 6)[i]
        step = (0, -1, 1, -2, 2, -3, 1, -1, 1)[i]
        source, landing = tokens_in.at[min(i, 7)], planes.at[slot]
        if i >= 7:
            rows = pl.ds((i - 7) * half_tokens, half_tokens)
            source, landing = tokens_in.at[7, rows], planes.at[slot, rows]
        return remote(source, landing, msend.at[i], mrecv.at[i], (along_z(step), x))

    def send_quarter(i):
        m = (right, far, left)[i]
        return remote(
            staged.at[:, pl.ds(pl.multiple_of(m * share, share), share)],
            quarters.at[i],
            fsend.at[i],
            frecv.at[i],
            (me, m),
        )

    square = (CHUNK_MAIN, CHUNK_MAIN)
    row = lax.broadcasted_iota(jnp.int32, square, 0)
    row_slot = (row & (MAIN - 1)).astype(f32)
    row_over = (MAIN + ((row & (MAIN - 1)) >> 3)).astype(f32)
    row_group = row & (GROUPS - 1)
    lane_group = lax.broadcasted_iota(jnp.int32, square, 1) & (GROUPS - 1)

    lane = lax.broadcasted_iota(jnp.int32, square, 1)

    def unsorted_row(r):
        return ((r >> 1) & (PER - 1)) * MAIN + (r & 1) * GROUPS + (r >> 4)

    sort = jnp.where(lane == unsorted_row(row), 1.0, 0.0).astype(bf16)
    unsort = jnp.where(row == unsorted_row(lane), 1.0, 0.0).astype(bf16)

    def spread(values):
        return jnp.broadcast_to(values[:, None, :], (PER, MAIN, LANES)).reshape(square)

    def dot(a, b):
        return jnp.dot(a, b, preferred_element_type=f32)

    def pick(i):
        rank = spread(routes[i, :PER])
        tokens = tokens_in[i]
        chosen = dot(jnp.where(rank == row_slot, 1.0, 0.0).astype(bf16), tokens)
        packed[i, :, :SPLIT] = chosen[:, :SPLIT].astype(bf16)
        packed[i, :, first:last] = chosen[:, SPLIT:].astype(bf16)
        wide = dot(jnp.where(rank == row_over, 1.0, 0.0).astype(bf16), tokens)
        for start, count, lane in ((0, SPLIT // LANES, SPLIT), (SPLIT, GROUPS, last)):
            tile = jnp.zeros(square, f32)
            for g in range(count):
                piece = wide[:, start + g * LANES : start + (g + 1) * LANES]
                tile = jnp.where(row_group == g, piece, tile)
            packed[i, :, lane : lane + LANES] = tile.astype(bf16)
        inbox[i, :MAIN] = packed[i, :MAIN]

        @pl.loop(1, PER)
        def _(k):
            exchange(i, k).start()

    def project(act, quarter):
        columns = pl.ds(pl.multiple_of(quarter * cols, cols), cols)
        return dot(act, down[:, columns])

    def compute(c):
        @pl.loop(1, PER)
        def _(k):
            exchange(c, k).wait_send()

        tails = jnp.concatenate(
            [inner[c, m, :, SPLIT:] for m in range(4)] + [inbox[c, :, last:]], axis=1
        )
        tails = dot(sort, tails).astype(bf16)

        def tail_piece(g, tile):
            return tails[g * CHUNK_OVER : (g + 1) * CHUNK_OVER, tile * LANES : (tile + 1) * LANES]

        per_share = share // LANES
        for m in range(4):
            extra = [tail_piece(g, m) for g in range(SPLIT // LANES)] + [
                tail_piece(m * per_share + g, 4) for g in range(per_share)
            ]
            body = jnp.concatenate(
                [
                    inner[c, m, :, :SPLIT],
                    inbox[c, :, first + m * share : first + (m + 1) * share],
                ],
                axis=1,
            )
            rows = jnp.concatenate([body, jnp.concatenate(extra, axis=1)], axis=0)
            part = dot(rows, gate_up[m * cols : (m + 1) * cols, :])
            if m == 0:
                acc[...] = part
            else:
                acc[...] += part
        gate, up = acc[:, :ff], acc[:, ff:]
        act = (gate / (1.0 + jnp.exp(-gate)) * up).astype(bf16)

        def keep_share(quarter, value):
            lanes = pl.ds(pl.multiple_of(first + quarter * share, LANES), share)
            packed[c, :, lanes] = value[:CHUNK_MAIN, SPLIT:].astype(bf16)
            staging = pl.ds(pl.multiple_of(quarter * share, share), share)
            staged[:CHUNK_OVER, staging] = value[CHUNK_MAIN:, SPLIT:].astype(bf16)

        value = project(act, far)
        to_far[c] = value[:, :SPLIT].astype(bf16)
        reduce(c, 0).start()
        reduce(c, 1).start()
        keep_share(far, value)
        value = project(act, right)
        to_right[c] = value[:, :SPLIT].astype(bf16)
        keep_share(right, value)
        value = project(act, left)
        to_left[c] = value[:, :SPLIT].astype(bf16)
        keep_share(left, value)
        value = project(act, x)
        own[c] = value[:, :SPLIT]
        keep_share(x, value)
        over = staged[:CHUNK_OVER, :]
        over = jnp.concatenate(
            [over[:, g * LANES : (g + 1) * LANES] for g in range(GROUPS)], axis=0
        )
        packed[c, :, last:] = dot(unsort, over).astype(bf16)

    def finish(c):
        reduce(c, 2).wait_recv()
        reduce(c, 3).wait_recv()
        value = (
            own[c] + from_left[c].astype(f32) + from_right[c].astype(f32)
        ).astype(bf16)
        packed[c, :, :SPLIT] = value[:CHUNK_MAIN]
        count = SPLIT // LANES
        over = jnp.concatenate(
            [value[CHUNK_MAIN:, g * LANES : (g + 1) * LANES] for g in range(count)]
            + [jnp.zeros(((GROUPS - count) * CHUNK_OVER, LANES), bf16)],
            axis=0,
        )
        packed[c, :, SPLIT:first] = dot(unsort, over).astype(bf16)
        returned[c, :MAIN] = packed[c, :MAIN]

        @pl.loop(1, PER)
        def _(k):
            give_back(c, k).start()

    def combine(c):
        @pl.loop(1, PER)
        def _(k):
            give_back(c, k).wait_recv()

        rank, weight = spread(routes[c, :PER]), spread(routes[c, PER:])
        rows = returned[c]
        whole = jnp.where(rank == row_slot, weight, 0.0).T
        over = jnp.where(rank == row_over, weight, 0.0).T
        high_part = whole.astype(bf16)
        low_part = (whole - high_part.astype(f32)).astype(bf16)
        mixed = dot(high_part, rows) + dot(low_part, rows)
        tiles = jnp.concatenate([rows[:, SPLIT:first], rows[:, last:]], axis=1)
        extra = []
        for g in range(GROUPS):
            picked = jnp.where(lane_group == g, over, 0.0)
            high_part = picked.astype(bf16)
            low_part = (picked - high_part.astype(f32)).astype(bf16)
            extra.append(dot(high_part, tiles) + dot(low_part, tiles))
        count = SPLIT // LANES
        inner_sum = mixed[:, :SPLIT] + jnp.concatenate(
            [extra[g][:, :LANES] for g in range(count)], axis=1
        )
        share_sum = mixed[:, first:last] + jnp.concatenate(
            [extra[g][:, LANES:] for g in range(GROUPS)], axis=1
        )

        @pl.when(c == 0)
        def _():
            total[:, :SPLIT] = inner_sum
            total[:, SPLIT:] = share_sum

        @pl.when((c >= 1) & (c <= DEPTH - 4))
        def _():
            ring(c + 2).wait_send()

        for side in (0, 1):

            @pl.when(c == DEPTH - 3 + side)
            def _():
                ring_far(side).wait_send()

        @pl.when(c > 0)
        def _():
            summed[:, :SPLIT] = inner_sum
            summed[:, SPLIT:] = share_sum

        for side in (0, 1):
            rows = slice(side * half_tokens, (side + 1) * half_tokens)

            @pl.when(c == 5 + side)
            def _():
                send_plane(7 + side).wait_recv()
                summed[rows] += planes[5 + side, rows].astype(f32)

        @pl.when(c == 4)
        def _():
            send_plane(6).wait_recv()
            summed[...] += planes[4].astype(f32)

        @pl.when(c > 0)
        def _():
            tokens_in[c] = summed[...].astype(bf16)

        for i in range(1, DEPTH):

            @pl.when(c == i)
            def _():
                send_plane(i).start()
                if i == 7:
                    send_plane(8).start()

    def order(p):
        late = lax.div(p + 4, DEPTH)
        return (1 - late) * p + late * (11 - p)

    pick(0)

    @pl.loop(0, DEPTH + 5)
    def _(t):
        @pl.when((t >= 1) & (t < DEPTH + 1))
        def _():
            c = order(t - 1)
            gather(c, 0).wait_recv()
            gather(c, 4).start()
            gather(c, 2).wait_recv()
            gather(c, 5).start()

        @pl.when(t < DEPTH)
        def _():
            c = order(t)

            @pl.loop(1, PER)
            def _(k):
                exchange(c, k).wait_recv()

            inner[c, x] = inbox[c, :, :inner_width]
            for i in (0, 2, 1, 3):
                gather(c, i).start()

        @pl.when((t >= DEPTH // 2) & (t + 1 < DEPTH))
        def _():
            i = order(t + 1)
            send_routes(i).wait_recv()
            pick(i)

        @pl.when(t == 2)
        def _():
            for copy in weights:
                copy.wait()

        @pl.when((t >= 2) & (t < DEPTH + 2))
        def _():
            c = order(t - 2)
            for i in (1, 3, 4, 5):
                gather(c, i).wait_recv()
            compute(c)

        @pl.when((t >= 3) & (t < DEPTH + 3))
        def _():
            c = order(t - 3)
            reduce(c, 0).wait_recv()
            to_right[c, :HALF_OUT] = (
                to_right[c, :HALF_OUT].astype(f32) + far_a[c].astype(f32)
            ).astype(bf16)
            reduce(c, 2).start()
            reduce(c, 1).wait_recv()
            to_left[c, HALF_OUT:] = (
                to_left[c, HALF_OUT:].astype(f32) + far_b[c].astype(f32)
            ).astype(bf16)
            reduce(c, 3).start()

        @pl.when((t >= 4) & (t < DEPTH + 4))
        def _():
            finish(order(t - 4))

        @pl.when(t >= 5)
        def _():
            combine(order(t - 5))

        @pl.when(t < 3)
        def _():
            for side in (0, 1):
                i = 2 * t + 1 + side
                ring(i).wait_recv()

                @pl.when(t < 2)
                def _():
                    ring(i + 2).start()

                @pl.when(t == 2)
                def _():
                    ring_far(side).start()

        @pl.when(t == 3)
        def _():
            for side in (0, 1):
                ring_far(side).wait_recv()

        @pl.when(t < DEPTH // 2)
        def _():
            i = order(t + 1)
            send_routes(i).wait_recv()
            pick(i)

    for i, slot in ((1, 1), (2, 2), (3, 3), (5, 7), (4, 0)):
        send_plane(i).wait_recv()
        total[...] += planes[slot].astype(f32)

    staged[...] = total[:, SPLIT:].astype(bf16)
    for i in range(3):
        send_quarter(i).start()
    out[:, :SPLIT] = (hidden[:, :SPLIT] + total[:, :SPLIT]).astype(bf16)
    mixture = total[:, pl.ds(pl.multiple_of(SPLIT + x * share, share), share)]
    for i in range(3):
        send_quarter(i).wait_recv()
        mixture += quarters[i].astype(f32)
    out[:, SPLIT:] = (hidden[:, SPLIT:] + mixture).astype(bf16)

    for i in (1, 2):
        ring(i, 0).wait_send()
    for i in range(3):
        send_quarter(i).wait_send()

    @pl.loop(1, DEPTH)
    def _(i):
        send_routes(i).wait_send()

    for i in range(1, DEPTH + 1):
        send_plane(i).wait_send()

    @pl.loop(0, DEPTH)
    def _(c):
        for i in range(6):
            gather(c, i).wait_send()
        for i in range(4):
            reduce(c, i).wait_send()

        @pl.loop(1, PER)
        def _(k):
            give_back(c, k).wait_send()


def experts(normed, routes, hidden, w_gate, w_up, w_down):
    tokens, wide = normed.shape
    cols = hidden.shape[1]
    ff, model_width = w_down.shape
    rows = CHUNK_ROWS
    width = wide + 2 * LANES
    bf16, f32 = jnp.bfloat16, jnp.float32
    dma = pltpu.SemaphoreType.DMA
    anywhere = pl.BlockSpec(memory_space=pl.ANY)
    onchip = pl.BlockSpec(memory_space=pltpu.VMEM)
    moved = pltpu.VMEM((DEPTH, rows, SPLIT), bf16)
    return pl.pallas_call(
        expert_kernel,
        out_shape=jax.ShapeDtypeStruct((tokens, cols), bf16),
        in_specs=[anywhere] * 2 + [onchip] + [anywhere] * 3,
        out_specs=onchip,
        scratch_shapes=[
            pltpu.VMEM((DEPTH, tokens, wide), bf16),
            pltpu.VMEM((DEPTH, 2 * PER, LANES), f32),
            pltpu.VMEM((DEPTH, CHUNK_MAIN, width), bf16),
            pltpu.VMEM((DEPTH, CHUNK_MAIN, width), bf16),
            pltpu.VMEM((DEPTH, 4, CHUNK_MAIN, SPLIT + LANES), bf16),
            pltpu.VMEM((model_width, 2 * ff), bf16),
            pltpu.VMEM((ff, model_width), bf16),
            pltpu.VMEM((rows, 2 * ff), f32),
            moved,
            moved,
            moved,
            pltpu.VMEM((DEPTH, rows, SPLIT), f32),
            pltpu.VMEM((DEPTH, HALF_OUT, SPLIT), bf16),
            pltpu.VMEM((DEPTH, rows - HALF_OUT, SPLIT), bf16),
            moved,
            moved,
            pltpu.VMEM((DEPTH, CHUNK_MAIN, width), bf16),
            pltpu.VMEM((DEPTH, tokens, wide), bf16),
            pltpu.VMEM((tokens, wide), f32),
            pltpu.VMEM((tokens, wide), f32),
            pltpu.VMEM((tokens, wide - SPLIT), bf16),
            pltpu.VMEM((3, tokens, cols - SPLIT), bf16),
            dma((5,)),
            dma((DEPTH + 1,)),
            dma((DEPTH + 1,)),
            dma((DEPTH,)),
            dma((DEPTH,)),
            dma((DEPTH, PER)),
            dma((DEPTH, PER)),
            dma((DEPTH, 6)),
            dma((DEPTH, 6)),
            dma((DEPTH, 4)),
            dma((DEPTH, 4)),
            dma((DEPTH, PER)),
            dma((DEPTH, PER)),
            dma((DEPTH + 1,)),
            dma((DEPTH + 1,)),
            dma((3,)),
            dma((3,)),
        ],
        compiler_params=pltpu.CompilerParams(
            collective_id=1, has_side_effects=True, vmem_limit_bytes=60 << 20
        ),
    )(normed, routes, hidden, w_gate, w_up, w_down)


def per_device(
    attn_heads, out_proj, residual, norm_gain, route_ids, route_weights, w_gate, w_up, w_down
):
    hidden, normed, routes = attention(
        attn_heads, out_proj, residual, norm_gain, route_ids, route_weights
    )
    return experts(normed, routes, hidden, w_gate[0], w_up[0], w_down[0])


def solution(mesh):
    placed = (
        P("expert", "tensor"),
        P("tensor", "expert"),
        P("expert", None),
        P(),
        P("expert", None),
        P("expert", None),
        P("expert", None, "tensor"),
        P("expert", None, "tensor"),
        P("expert", "tensor", None),
    )
    return jax.shard_map(
        per_device, mesh=mesh, in_specs=placed, out_specs=P("expert", "tensor"), check_vma=False
    )
```

```python
import jax
import jax.numpy as jnp
from jax import lax
from jax.experimental import pallas as pl
from jax.experimental.pallas import tpu as pltpu
from jax.sharding import PartitionSpec as P

MESH = pl.DeviceIdType.MESH
EXPERTS = 64
RING = 16
ROWS_Y = EXPERTS // RING
MAIN = 16
OVER = 2
LANES = 128
GROUPS = 8
SPLIT = 768
DEPTH = 8
PER = 8
CHUNK_MAIN = PER * MAIN
CHUNK_OVER = PER * OVER
CHUNK_ROWS = CHUNK_MAIN + CHUNK_OVER
HALF_IN = CHUNK_MAIN // 2
HALF_OUT = CHUNK_ROWS // 2 // 16 * 16


def attention_kernel(
    heads_hbm, proj_hbm, residual_hbm, gain_hbm, route_ids, route_weights,
    hidden_out, normed_out, routes_out,
    shard, sibling_shard, weight, heads, to_far, to_right, to_left, own,
    far_a, far_b, from_left, from_right, mine, arrived, residual, gain, squares,
    shared, shared_residual, shared_gain,
    local_sem, shard_sem, zsend, zrecv, csend, crecv, hsend, hrecv, rsend, rrecv, wsend, wrecv, nsend, nrecv,
    ssend, srecv,
):
    me = lax.axis_index("expert")
    x = lax.axis_index("tensor")
    y, zc = lax.div(me, RING), lax.rem(me, RING)
    core, z = lax.rem(zc, 2), lax.div(zc, 2)
    depth = RING // 2
    right, left, far = lax.rem(x + 1, 4), lax.rem(x + 3, 4), lax.rem(x + 2, 4)
    sibling = me + 1 - 2 * core
    cols = from_left.shape[1]
    half = weight.shape[1] // 2
    tokens = heads.shape[1]

    def along_z(step):
        return y * RING + lax.rem(z + depth + step, depth) * 2 + core

    def along_y(step):
        return lax.rem(y + step, ROWS_Y) * RING + zc

    partner = (x * RING + zc, y)
    local = [
        pltpu.make_async_copy(proj_hbm, shard, local_sem.at[0]),
        pltpu.make_async_copy(heads_hbm, heads.at[y], local_sem.at[1]),
        pltpu.make_async_copy(
            residual_hbm.at[:, pl.ds(pl.multiple_of(x * cols, cols), cols)], residual, local_sem.at[2]
        ),
        pltpu.make_async_copy(
            gain_hbm.at[:, pl.ds(pl.multiple_of(x * cols, cols), cols)], gain, local_sem.at[3]
        ),
    ]
    share = cols - SPLIT
    for m in range(4):
        local.append(
            pltpu.make_async_copy(
                residual_hbm.at[:, pl.ds(m * cols + SPLIT, share)],
                shared_residual.at[:, pl.ds(m * share, share)],
                local_sem.at[4 + m],
            )
        )
        local.append(
            pltpu.make_async_copy(
                gain_hbm.at[:, pl.ds(m * cols + SPLIT, share)],
                shared_gain.at[:, pl.ds(m * share, share)],
                local_sem.at[8 + m],
            )
        )
    for copy in local:
        copy.start()

    barrier = pltpu.get_barrier_semaphore()
    for device in (sibling, along_z(1), along_z(-1), along_y(1), along_y(2), along_y(3)):
        pl.semaphore_signal(barrier, inc=1, device_id=(device, x), device_id_type=MESH)
    for m in (right, left, far):
        pl.semaphore_signal(barrier, inc=1, device_id=(me, m), device_id_type=MESH)

    @pl.when(x != y)
    def _():
        pl.semaphore_signal(barrier, inc=1, device_id=partner, device_id_type=MESH)
        pl.semaphore_wait(barrier, 10)

    @pl.when(x == y)
    def _():
        pl.semaphore_wait(barrier, 9)

    def remote(source, landing, send, recv, device):
        return pltpu.make_async_remote_copy(
            src_ref=source,
            dst_ref=landing,
            send_sem=send,
            recv_sem=recv,
            device_id=device,
            device_id_type=MESH,
        )

    swap_shard = remote(
        shard.at[:, pl.ds(pl.multiple_of((1 - core) * half, half), half)],
        sibling_shard,
        shard_sem.at[0],
        shard_sem.at[1],
        (sibling, x),
    )
    local[0].wait()
    swap_shard.start()
    local[1].wait()

    def share_heads(i):
        return remote(heads.at[y], heads.at[y], hsend.at[i], hrecv.at[i], (along_y(i + 1), x))

    for i in (1, 0, 2):
        share_heads(i).start()

    def piece(owner, part):
        start = core * half + (half // 2 if part == 2 else 0)
        count = half if part == 0 else half // 2
        return weight.at[owner, pl.ds(pl.multiple_of(start, half // 2), count)]

    def ring(direction, s):
        offset = -(s - 1) if direction == 0 else s - 1
        ref = piece(
            lax.rem(z + depth + offset, depth), (1 + direction) if s == depth // 2 else 0
        )
        target = along_z(1 if direction == 0 else -1)
        return remote(ref, ref, zsend.at[direction, s - 1], zrecv.at[direction, s - 1], (target, x))

    def across(direction, s):
        offset = -s if direction == 0 else s
        ref = piece(
            lax.rem(z + depth + offset, depth), (1 + direction) if s == depth // 2 else 0
        )
        i = 5 * direction + s
        return remote(ref, ref, csend.at[i], crecv.at[i], (sibling, x))

    width = shard.shape[0]
    row = lax.broadcasted_iota(jnp.int32, (LANES, width), 0)
    lane = lax.broadcasted_iota(jnp.int32, (LANES, width), 1)
    put_own = (row == lane + width * core).astype(jnp.bfloat16)
    put_other = (row == lane + width * (1 - core)).astype(jnp.bfloat16)
    swap_shard.wait_recv()
    both = jnp.dot(
        put_own,
        shard[:, pl.ds(pl.multiple_of(core * half, half), half)],
        preferred_element_type=jnp.float32,
    ) + jnp.dot(put_other, sibling_shard[...], preferred_element_type=jnp.float32)
    both = both.T
    weight[z, pl.ds(pl.multiple_of(core * half, half), half)] = both.astype(jnp.bfloat16)
    ring(0, 1).start()
    ring(1, 1).start()
    across(0, 0).start()
    square = (tokens, LANES)
    row = lax.broadcasted_iota(jnp.int32, square, 0)
    earlier = jnp.where(row < lax.broadcasted_iota(jnp.int32, square, 1), 1.0, 0.0)
    ids = route_ids[...]
    ahead_z = (((ids & (RING - 1)) >> 1) + depth - z) & (depth - 1)
    chunk = jnp.where(
        ahead_z == 0, 0, jnp.where(ahead_z <= depth // 2, 2 * ahead_z - 1, 2 * (depth - ahead_z))
    )
    ahead_y = ((ids >> 4) + ROWS_Y - y) & (ROWS_Y - 1)
    relative = chunk * PER + ahead_y * 2 + ((ids + 2 - core) & 1)
    shares = route_weights[...] / jnp.sum(route_weights[...], axis=0, keepdims=True)
    chosen = jnp.zeros(square, jnp.float32)
    scaled = jnp.zeros(square, jnp.float32)
    for k in range(ids.shape[0]):
        hit = row == relative[k : k + 1]
        chosen = jnp.where(hit, 1.0, chosen)
        scaled = jnp.where(hit, shares[k : k + 1], scaled)
    rank = jnp.dot(
        chosen.astype(jnp.bfloat16),
        earlier.astype(jnp.bfloat16),
        preferred_element_type=jnp.float32,
    )
    rank = jnp.where(chosen > 0, rank, -1.0)
    for i in range(depth):
        routes_out[i, :PER] = rank[i * PER : (i + 1) * PER]
        routes_out[i, PER:] = scaled[i * PER : (i + 1) * PER]

    for s in range(1, depth // 2 + 1):
        for direction in (0, 1):
            ring(direction, s).wait_recv()
            if s < depth // 2:
                ring(direction, s + 1).start()
            across(direction, s).start()
    handed = [(0, 0)] + [(d, s) for s in range(1, depth // 2 + 1) for d in (0, 1)]
    for i in (0, 2, 1):
        share_heads(i).wait_recv()
    for d, s in handed:
        across(d, s).wait_recv()

    def partial(block):
        return jnp.concatenate(
            [
                jnp.dot(
                    heads[block],
                    jnp.concatenate([weight[i], weight[i + 1]], axis=1),
                    preferred_element_type=jnp.float32,
                )
                for i in range(0, RING // 2, 2)
            ],
            axis=1,
        )

    part = tokens // 2

    def reduce(i):
        rows = pl.ds((0, part, part, 0, 0, part)[i], part)
        source = (to_far, to_far, to_right, to_left, to_right, to_left)[i].at[rows]
        landing = (
            far_a,
            far_b,
            from_left.at[rows],
            from_right.at[rows],
            from_left.at[rows],
            from_right.at[rows],
        )[i]
        target = (right, left)[i % 2]
        return remote(source, landing, rsend.at[i], rrecv.at[i], (me, target))

    def exchange(i):
        rows = pl.ds(i * part, part)
        return remote(mine.at[rows], arrived.at[rows], wsend.at[i], wrecv.at[i], partner)

    to_far[...] = partial(far).astype(jnp.bfloat16)
    reduce(0).start()
    reduce(1).start()
    via_right = partial(right)
    to_right[part:] = via_right[part:].astype(jnp.bfloat16)
    reduce(2).start()
    via_left = partial(left)
    to_left[:part] = via_left[:part].astype(jnp.bfloat16)
    reduce(3).start()
    reduce(0).wait_recv()
    to_right[:part] = (via_right[:part] + far_a[...].astype(jnp.float32)).astype(jnp.bfloat16)
    reduce(4).start()
    reduce(1).wait_recv()
    to_left[part:] = (via_left[part:] + far_b[...].astype(jnp.float32)).astype(jnp.bfloat16)
    reduce(5).start()
    own[...] = partial(x)
    for i in range(2):
        rows = slice(i * part, (i + 1) * part)
        reduce((4, 2)[i]).wait_recv()
        reduce((3, 5)[i]).wait_recv()
        mine[rows] = (
            own[rows]
            + from_left[rows].astype(jnp.float32)
            + from_right[rows].astype(jnp.float32)
        ).astype(jnp.bfloat16)

        @pl.when(x != y)
        def _():
            exchange(i).start()

    @pl.when(x != y)
    def _():
        exchange(0).wait_recv()
        exchange(1).wait_recv()

    @pl.when(x == y)
    def _():
        arrived[...] = mine[...]

    shared[x] = arrived[:, SPLIT:]

    def share_features(i):
        return remote(
            shared.at[x], shared.at[x], ssend.at[i], srecv.at[i], (me, (right, far, left)[i])
        )

    for i in range(3):
        share_features(i).start()
    for copy in local[2:]:
        copy.wait()
    hidden = residual[...].astype(jnp.float32) + arrived[...].astype(jnp.float32)
    hidden_out[...] = hidden
    squares[0] = jnp.broadcast_to(
        jnp.sum(hidden * hidden, axis=-1, keepdims=True), square
    ).T[:PER]

    def share_squares(i):
        return remote(
            squares.at[0], squares.at[i + 1], nsend.at[i], nrecv.at[i], (me, (right, far, left)[i])
        )

    for i in range(3):
        share_squares(i).start()
    for i in range(3):
        share_squares(i).wait_recv()
        share_features(i).wait_recv()
    mean = (squares[0] + squares[1] + squares[2] + squares[3]) / (4 * cols)
    scale = jnp.broadcast_to(lax.rsqrt(mean + 1e-06)[:1], square).T[:, :1]
    normed_out[:, :SPLIT] = (hidden[:, :SPLIT] * scale * gain[:, :SPLIT]).astype(jnp.bfloat16)
    for m in range(4):
        lanes = slice(m * share, (m + 1) * share)
        value = shared_residual[:, lanes].astype(jnp.float32) + shared[m].astype(jnp.float32)
        normed_out[:, SPLIT + m * share : SPLIT + (m + 1) * share] = (
            value * scale * shared_gain[:, lanes]
        ).astype(jnp.bfloat16)

    @pl.when(x != y)
    def _():
        exchange(0).wait_send()
        exchange(1).wait_send()

    swap_shard.wait_send()
    for i in range(3):
        share_heads(i).wait_send()
        share_squares(i).wait_send()
        share_features(i).wait_send()
    for d, s in handed:
        across(d, s).wait_send()
    for s in range(1, depth // 2 + 1):
        for direction in (0, 1):
            ring(direction, s).wait_send()
    for i in range(6):
        reduce(i).wait_send()


def attention(attn_heads, out_proj, residual, norm_gain, route_ids, route_weights):
    tokens, depth = attn_heads.shape
    cols = residual.shape[1] // 4
    bf16, f32 = jnp.bfloat16, jnp.float32
    dma = pltpu.SemaphoreType.DMA
    anywhere = pl.BlockSpec(memory_space=pl.ANY)
    onchip = pl.BlockSpec(memory_space=pltpu.VMEM)
    block = pltpu.VMEM((tokens, cols), bf16)
    return pl.pallas_call(
        attention_kernel,
        out_shape=(
            jax.ShapeDtypeStruct((tokens, cols), f32),
            jax.ShapeDtypeStruct((tokens, SPLIT + 4 * (cols - SPLIT)), bf16),
            jax.ShapeDtypeStruct((DEPTH, 2 * PER, tokens), f32),
        ),
        in_specs=[anywhere] * 4 + [onchip] * 2,
        out_specs=(onchip, onchip, onchip),
        scratch_shapes=[
            pltpu.VMEM(out_proj.shape, bf16),
            pltpu.VMEM((out_proj.shape[0], depth // 2), bf16),
            pltpu.VMEM((RING // 2, depth, LANES), bf16),
            pltpu.VMEM((ROWS_Y, tokens, depth), bf16),
            block,
            block,
            block,
            pltpu.VMEM((tokens, cols), f32),
            pltpu.VMEM((tokens // 2, cols), bf16),
            pltpu.VMEM((tokens // 2, cols), bf16),
            block,
            block,
            block,
            block,
            block,
            pltpu.VMEM((1, cols), f32),
            pltpu.VMEM((4, PER, LANES), f32),
            pltpu.VMEM((4, tokens, cols - SPLIT), bf16),
            pltpu.VMEM((tokens, 4 * (cols - SPLIT)), bf16),
            pltpu.VMEM((1, 4 * (cols - SPLIT)), f32),
            dma((12,)),
            dma((2,)),
            dma((2, 4)),
            dma((2, 4)),
            dma((10,)),
            dma((10,)),
            dma((3,)),
            dma((3,)),
            dma((6,)),
            dma((6,)),
            dma((2,)),
            dma((2,)),
            dma((3,)),
            dma((3,)),
            dma((3,)),
            dma((3,)),
        ],
        compiler_params=pltpu.CompilerParams(
            collective_id=2, has_side_effects=True, vmem_limit_bytes=60 << 20
        ),
    )(attn_heads, out_proj, residual, norm_gain[None, :], route_ids, route_weights)


def expert_kernel(
    normed, routes_in, hidden, gate_hbm, up_hbm, down_hbm, out,
    tokens_in, routes, packed, inbox, inner, gate_up, down, acc,
    to_far, to_right, to_left, own, far_a, far_b, from_left, from_right,
    returned, planes, total, summed, staged, quarters,
    local_sem, zsend, zrecv, tsend, trecv, ysend, yrecv, asend, arecv,
    rsend, rrecv, bsend, brecv, msend, mrecv, fsend, frecv,
):
    me = lax.axis_index("expert")
    x = lax.axis_index("tensor")
    y, zc = lax.div(me, RING), lax.rem(me, RING)
    core, z = lax.rem(zc, 2), lax.div(zc, 2)
    right, left, far = lax.rem(x + 1, 4), lax.rem(x + 3, 4), lax.rem(x + 2, 4)
    ff = gate_hbm.shape[1]
    cols = hidden.shape[1]
    share = cols - SPLIT
    inner_width = SPLIT + LANES
    first = inner_width
    last = first + 4 * share
    bf16, f32 = jnp.bfloat16, jnp.float32

    def along_z(step):
        return y * RING + lax.rem(z + DEPTH + step, DEPTH) * 2 + core

    def distance(i):
        odd = lax.rem(i, 2)
        return lax.rem(odd * lax.div(i + 1, 2) + (1 - odd) * (DEPTH - lax.div(i, 2)), DEPTH)

    def plane(dy, dc):
        return lax.rem(y + ROWS_Y + dy, ROWS_Y) * RING + z * 2 + lax.rem(core + dc, 2)

    def remote(source, landing, send, recv, device):
        return pltpu.make_async_remote_copy(
            src_ref=source,
            dst_ref=landing,
            send_sem=send,
            recv_sem=recv,
            device_id=device,
            device_id_type=MESH,
        )

    weights = [
        pltpu.make_async_copy(gate_hbm, gate_up.at[:, pl.ds(0, ff)], local_sem.at[0]),
        pltpu.make_async_copy(up_hbm, gate_up.at[:, pl.ds(ff, ff)], local_sem.at[1]),
        pltpu.make_async_copy(down_hbm, down, local_sem.at[2]),
    ]
    load_tokens = pltpu.make_async_copy(normed, tokens_in.at[0], local_sem.at[3])
    load_routes = pltpu.make_async_copy(routes_in.at[0], routes.at[0], local_sem.at[4])
    load_tokens.start()
    load_routes.start()
    for copy in weights:
        copy.start()

    barrier = pltpu.get_barrier_semaphore()

    @pl.loop(1, DEPTH)
    def _(i):
        pl.semaphore_signal(barrier, inc=1, device_id=(along_z(i), x), device_id_type=MESH)
        pl.semaphore_signal(
            barrier,
            inc=1,
            device_id=(plane(lax.div(i, 2), lax.rem(i, 2)), x),
            device_id_type=MESH,
        )

    for m in (right, far, left):
        pl.semaphore_signal(barrier, inc=1, device_id=(me, m), device_id_type=MESH)
    pl.semaphore_wait(barrier, 2 * (DEPTH - 1) + 3)

    def block(k):
        return pl.ds(pl.multiple_of(k * MAIN, MAIN), MAIN)

    def send_routes(i):
        return remote(
            routes_in.at[i], routes.at[i], tsend.at[i], trecv.at[i], (along_z(distance(i)), x)
        )

    def ring(i, before=None):
        before = lax.rem(i + DEPTH - 2, DEPTH) if before is None else before
        return remote(
            tokens_in.at[before],
            tokens_in.at[i],
            zsend.at[i],
            zrecv.at[i],
            (along_z(2 * lax.rem(i, 2) - 1), x),
        )

    middle = tokens_in.shape[1] // 2

    def ring_far(side):
        rows = pl.ds(side * middle, middle)
        return remote(
            tokens_in.at[DEPTH - 3 + side, rows],
            tokens_in.at[DEPTH - 1, rows],
            zsend.at[DEPTH - 1 + side],
            zrecv.at[DEPTH - 1 + side],
            (along_z(1 - 2 * side), x),
        )

    load_tokens.wait()
    ring(1, 0).start()
    ring(2, 0).start()

    @pl.loop(1, DEPTH)
    def _(i):
        send_routes(i).start()

    load_routes.wait()

    def exchange(i, k):
        return remote(
            packed.at[i, block(k)],
            inbox.at[i, block(k)],
            ysend.at[i, k],
            yrecv.at[i, k],
            (plane(lax.div(k, 2), lax.rem(k, 2)), x),
        )

    def give_back(i, k):
        return remote(
            packed.at[i, block(k)],
            returned.at[i, block(k)],
            bsend.at[i, k],
            brecv.at[i, k],
            (plane(-lax.div(k, 2), lax.rem(k, 2)), x),
        )

    low, high = pl.ds(0, HALF_IN), pl.ds(HALF_IN, HALF_IN)

    def gather(c, i):
        owner = (x, x, x, x, left, right)[i]
        part = (low, high, high, low, low, high)[i]
        target = (right, right, left, left, right, left)[i]
        ref = inner.at[c, owner, part]
        return remote(ref, ref, asend.at[c, i], arecv.at[c, i], (me, target))

    head, tail = pl.ds(0, HALF_OUT), pl.ds(HALF_OUT, CHUNK_ROWS - HALF_OUT)

    def reduce(c, i):
        rows = (head, tail, tail, head, head, tail)[i]
        source = (to_far, to_far, to_right, to_left, to_right, to_left)[i].at[c, rows]
        landing = (
            far_a.at[c],
            far_b.at[c],
            from_left.at[c, rows],
            from_right.at[c, rows],
            from_left.at[c, rows],
            from_right.at[c, rows],
        )[i]
        target = (right, left)[i % 2]
        return remote(source, landing, rsend.at[c, i], rrecv.at[c, i], (me, target))

    half_tokens = tokens_in.shape[1] // 2

    def send_plane(i):
        slot = (0, 1, 2, 3, 0, 7, 4, 5, 6)[i]
        step = (0, -1, 1, -2, 2, -3, 1, -1, 1)[i]
        source, landing = tokens_in.at[min(i, 7)], planes.at[slot]
        if i >= 7:
            rows = pl.ds((i - 7) * half_tokens, half_tokens)
            source, landing = tokens_in.at[7, rows], planes.at[slot, rows]
        return remote(source, landing, msend.at[i], mrecv.at[i], (along_z(step), x))

    def send_quarter(i):
        m = (right, far, left)[i]
        return remote(
            staged.at[:, pl.ds(pl.multiple_of(m * share, share), share)],
            quarters.at[i],
            fsend.at[i],
            frecv.at[i],
            (me, m),
        )

    square = (CHUNK_MAIN, CHUNK_MAIN)
    row = lax.broadcasted_iota(jnp.int32, square, 0)
    row_slot = (row & (MAIN - 1)).astype(f32)
    row_over = (MAIN + ((row & (MAIN - 1)) >> 3)).astype(f32)
    row_group = row & (GROUPS - 1)
    lane_group = lax.broadcasted_iota(jnp.int32, square, 1) & (GROUPS - 1)

    lane = lax.broadcasted_iota(jnp.int32, square, 1)

    def unsorted_row(r):
        return ((r >> 1) & (PER - 1)) * MAIN + (r & 1) * GROUPS + (r >> 4)

    sort = jnp.where(lane == unsorted_row(row), 1.0, 0.0).astype(bf16)
    unsort = jnp.where(row == unsorted_row(lane), 1.0, 0.0).astype(bf16)

    def spread(values):
        return jnp.broadcast_to(values[:, None, :], (PER, MAIN, LANES)).reshape(square)

    def dot(a, b):
        return jnp.dot(a, b, preferred_element_type=f32)

    def pick(i):
        rank = spread(routes[i, :PER])
        tokens = tokens_in[i]
        chosen = dot(jnp.where(rank == row_slot, 1.0, 0.0).astype(bf16), tokens)
        packed[i, :, :SPLIT] = chosen[:, :SPLIT].astype(bf16)
        packed[i, :, first:last] = chosen[:, SPLIT:].astype(bf16)
        wide = dot(jnp.where(rank == row_over, 1.0, 0.0).astype(bf16), tokens)
        for start, count, lane in ((0, SPLIT // LANES, SPLIT), (SPLIT, GROUPS, last)):
            tile = jnp.zeros(square, f32)
            for g in range(count):
                piece = wide[:, start + g * LANES : start + (g + 1) * LANES]
                tile = jnp.where(row_group == g, piece, tile)
            packed[i, :, lane : lane + LANES] = tile.astype(bf16)
        inbox[i, :MAIN] = packed[i, :MAIN]

        @pl.loop(1, PER)
        def _(k):
            exchange(i, k).start()

    def project(act, quarter):
        columns = pl.ds(pl.multiple_of(quarter * cols, cols), cols)
        return dot(act, down[:, columns])

    def compute(c):
        @pl.loop(1, PER)
        def _(k):
            exchange(c, k).wait_send()

        tails = jnp.concatenate(
            [inner[c, m, :, SPLIT:] for m in range(4)] + [inbox[c, :, last:]], axis=1
        )
        tails = dot(sort, tails).astype(bf16)

        def tail_piece(g, tile):
            return tails[g * CHUNK_OVER : (g + 1) * CHUNK_OVER, tile * LANES : (tile + 1) * LANES]

        per_share = share // LANES
        for m in range(4):
            extra = [tail_piece(g, m) for g in range(SPLIT // LANES)] + [
                tail_piece(m * per_share + g, 4) for g in range(per_share)
            ]
            body = jnp.concatenate(
                [
                    inner[c, m, :, :SPLIT],
                    inbox[c, :, first + m * share : first + (m + 1) * share],
                ],
                axis=1,
            )
            rows = jnp.concatenate([body, jnp.concatenate(extra, axis=1)], axis=0)
            part = dot(rows, gate_up[m * cols : (m + 1) * cols, :])
            if m == 0:
                acc[...] = part
            else:
                acc[...] += part
        gate, up = acc[:, :ff], acc[:, ff:]
        act = (gate / (1.0 + jnp.exp(-gate)) * up).astype(bf16)

        def keep_share(quarter, value):
            lanes = pl.ds(pl.multiple_of(first + quarter * share, LANES), share)
            packed[c, :, lanes] = value[:CHUNK_MAIN, SPLIT:].astype(bf16)
            staging = pl.ds(pl.multiple_of(quarter * share, share), share)
            staged[:CHUNK_OVER, staging] = value[CHUNK_MAIN:, SPLIT:].astype(bf16)

        value = project(act, far)
        to_far[c] = value[:, :SPLIT].astype(bf16)
        reduce(c, 0).start()
        reduce(c, 1).start()
        keep_share(far, value)
        value = project(act, right)
        to_right[c] = value[:, :SPLIT].astype(bf16)
        reduce(c, 2).start()
        keep_share(right, value)
        value = project(act, left)
        to_left[c] = value[:, :SPLIT].astype(bf16)
        reduce(c, 3).start()
        keep_share(left, value)
        value = project(act, x)
        own[c] = value[:, :SPLIT]
        keep_share(x, value)
        over = staged[:CHUNK_OVER, :]
        over = jnp.concatenate(
            [over[:, g * LANES : (g + 1) * LANES] for g in range(GROUPS)], axis=0
        )
        packed[c, :, last:] = dot(unsort, over).astype(bf16)

    def finish(c):
        for i in (2, 3, 4, 5):
            reduce(c, i).wait_recv()
        value = (
            own[c] + from_left[c].astype(f32) + from_right[c].astype(f32)
        ).astype(bf16)
        packed[c, :, :SPLIT] = value[:CHUNK_MAIN]
        count = SPLIT // LANES
        over = jnp.concatenate(
            [value[CHUNK_MAIN:, g * LANES : (g + 1) * LANES] for g in range(count)]
            + [jnp.zeros(((GROUPS - count) * CHUNK_OVER, LANES), bf16)],
            axis=0,
        )
        packed[c, :, SPLIT:first] = dot(unsort, over).astype(bf16)
        returned[c, :MAIN] = packed[c, :MAIN]

        @pl.loop(1, PER)
        def _(k):
            give_back(c, k).start()

    def combine(c):
        @pl.loop(1, PER)
        def _(k):
            give_back(c, k).wait_recv()

        rank, weight = spread(routes[c, :PER]), spread(routes[c, PER:])
        rows = returned[c]
        whole = jnp.where(rank == row_slot, weight, 0.0).T
        over = jnp.where(rank == row_over, weight, 0.0).T
        high_part = whole.astype(bf16)
        low_part = (whole - high_part.astype(f32)).astype(bf16)
        mixed = dot(high_part, rows) + dot(low_part, rows)
        tiles = jnp.concatenate([rows[:, SPLIT:first], rows[:, last:]], axis=1)
        extra = []
        for g in range(GROUPS):
            picked = jnp.where(lane_group == g, over, 0.0)
            high_part = picked.astype(bf16)
            low_part = (picked - high_part.astype(f32)).astype(bf16)
            extra.append(dot(high_part, tiles) + dot(low_part, tiles))
        count = SPLIT // LANES
        inner_sum = mixed[:, :SPLIT] + jnp.concatenate(
            [extra[g][:, :LANES] for g in range(count)], axis=1
        )
        share_sum = mixed[:, first:last] + jnp.concatenate(
            [extra[g][:, LANES:] for g in range(GROUPS)], axis=1
        )

        @pl.when(c == 0)
        def _():
            total[:, :SPLIT] = inner_sum
            total[:, SPLIT:] = share_sum

        @pl.when((c >= 1) & (c <= DEPTH - 4))
        def _():
            ring(c + 2).wait_send()

        for side in (0, 1):

            @pl.when(c == DEPTH - 3 + side)
            def _():
                ring_far(side).wait_send()

        @pl.when(c > 0)
        def _():
            summed[:, :SPLIT] = inner_sum
            summed[:, SPLIT:] = share_sum

        for side in (0, 1):
            rows = slice(side * half_tokens, (side + 1) * half_tokens)

            @pl.when(c == 5 + side)
            def _():
                send_plane(7 + side).wait_recv()
                summed[rows] += planes[5 + side, rows].astype(f32)

        @pl.when(c == 4)
        def _():
            send_plane(6).wait_recv()
            summed[...] += planes[4].astype(f32)

        @pl.when(c > 0)
        def _():
            tokens_in[c] = summed[...].astype(bf16)

        for i in range(1, DEPTH):

            @pl.when(c == i)
            def _():
                send_plane(i).start()
                if i == 7:
                    send_plane(8).start()

    def order(p):
        late = lax.div(p + 4, DEPTH)
        return (1 - late) * p + late * (11 - p)

    pick(0)

    @pl.loop(0, DEPTH + 5)
    def _(t):
        @pl.when((t >= 1) & (t < DEPTH + 1))
        def _():
            c = order(t - 1)
            gather(c, 0).wait_recv()
            gather(c, 4).start()
            gather(c, 2).wait_recv()
            gather(c, 5).start()

        @pl.when(t < DEPTH)
        def _():
            c = order(t)

            @pl.loop(1, PER)
            def _(k):
                exchange(c, k).wait_recv()

            inner[c, x] = inbox[c, :, :inner_width]
            for i in (0, 2, 1, 3):
                gather(c, i).start()

        @pl.when((t >= DEPTH // 2) & (t + 1 < DEPTH))
        def _():
            i = order(t + 1)
            send_routes(i).wait_recv()
            pick(i)

        @pl.when(t == 2)
        def _():
            for copy in weights:
                copy.wait()

        @pl.when((t >= 2) & (t < DEPTH + 2))
        def _():
            c = order(t - 2)
            for i in (1, 3, 4, 5):
                gather(c, i).wait_recv()
            compute(c)

        @pl.when((t >= 3) & (t < DEPTH + 3))
        def _():
            c = order(t - 3)
            reduce(c, 0).wait_recv()
            to_right[c, :HALF_OUT] = (
                to_right[c, :HALF_OUT].astype(f32) + far_a[c].astype(f32)
            ).astype(bf16)
            reduce(c, 4).start()
            reduce(c, 1).wait_recv()
            to_left[c, HALF_OUT:] = (
                to_left[c, HALF_OUT:].astype(f32) + far_b[c].astype(f32)
            ).astype(bf16)
            reduce(c, 5).start()

        @pl.when((t >= 4) & (t < DEPTH + 4))
        def _():
            finish(order(t - 4))

        @pl.when(t >= 5)
        def _():
            combine(order(t - 5))

        @pl.when(t < 3)
        def _():
            for side in (0, 1):
                i = 2 * t + 1 + side
                ring(i).wait_recv()

                @pl.when(t < 2)
                def _():
                    ring(i + 2).start()

                @pl.when(t == 2)
                def _():
                    ring_far(side).start()

        @pl.when(t == 3)
        def _():
            for side in (0, 1):
                ring_far(side).wait_recv()

        @pl.when(t < DEPTH // 2)
        def _():
            i = order(t + 1)
            send_routes(i).wait_recv()
            pick(i)

    for i, slot in ((1, 1), (2, 2), (3, 3), (5, 7), (4, 0)):
        send_plane(i).wait_recv()
        total[...] += planes[slot].astype(f32)

    staged[...] = total[:, SPLIT:].astype(bf16)
    for i in range(3):
        send_quarter(i).start()
    out[:, :SPLIT] = hidden[:, :SPLIT] + total[:, :SPLIT]
    mixture = total[:, pl.ds(pl.multiple_of(SPLIT + x * share, share), share)]
    for i in range(3):
        send_quarter(i).wait_recv()
        mixture += quarters[i].astype(f32)
    out[:, SPLIT:] = hidden[:, SPLIT:] + mixture

    for i in (1, 2):
        ring(i, 0).wait_send()
    for i in range(3):
        send_quarter(i).wait_send()

    @pl.loop(1, DEPTH)
    def _(i):
        send_routes(i).wait_send()

    for i in range(1, DEPTH + 1):
        send_plane(i).wait_send()

    @pl.loop(0, DEPTH)
    def _(c):
        for i in range(6):
            gather(c, i).wait_send()
            reduce(c, i).wait_send()

        @pl.loop(1, PER)
        def _(k):
            give_back(c, k).wait_send()


def experts(normed, routes, hidden, w_gate, w_up, w_down):
    tokens, wide = normed.shape
    cols = hidden.shape[1]
    ff, model_width = w_down.shape
    rows = CHUNK_ROWS
    width = wide + 2 * LANES
    bf16, f32 = jnp.bfloat16, jnp.float32
    dma = pltpu.SemaphoreType.DMA
    anywhere = pl.BlockSpec(memory_space=pl.ANY)
    onchip = pl.BlockSpec(memory_space=pltpu.VMEM)
    moved = pltpu.VMEM((DEPTH, rows, SPLIT), bf16)
    return pl.pallas_call(
        expert_kernel,
        out_shape=jax.ShapeDtypeStruct((tokens, cols), f32),
        in_specs=[anywhere] * 2 + [onchip] + [anywhere] * 3,
        out_specs=onchip,
        scratch_shapes=[
            pltpu.VMEM((DEPTH, tokens, wide), bf16),
            pltpu.VMEM((DEPTH, 2 * PER, LANES), f32),
            pltpu.VMEM((DEPTH, CHUNK_MAIN, width), bf16),
            pltpu.VMEM((DEPTH, CHUNK_MAIN, width), bf16),
            pltpu.VMEM((DEPTH, 4, CHUNK_MAIN, SPLIT + LANES), bf16),
            pltpu.VMEM((model_width, 2 * ff), bf16),
            pltpu.VMEM((ff, model_width), bf16),
            pltpu.VMEM((rows, 2 * ff), f32),
            moved,
            moved,
            moved,
            pltpu.VMEM((DEPTH, rows, SPLIT), f32),
            pltpu.VMEM((DEPTH, HALF_OUT, SPLIT), bf16),
            pltpu.VMEM((DEPTH, rows - HALF_OUT, SPLIT), bf16),
            moved,
            moved,
            pltpu.VMEM((DEPTH, CHUNK_MAIN, width), bf16),
            pltpu.VMEM((DEPTH, tokens, wide), bf16),
            pltpu.VMEM((tokens, wide), f32),
            pltpu.VMEM((tokens, wide), f32),
            pltpu.VMEM((tokens, wide - SPLIT), bf16),
            pltpu.VMEM((3, tokens, cols - SPLIT), bf16),
            dma((5,)),
            dma((DEPTH + 1,)),
            dma((DEPTH + 1,)),
            dma((DEPTH,)),
            dma((DEPTH,)),
            dma((DEPTH, PER)),
            dma((DEPTH, PER)),
            dma((DEPTH, 6)),
            dma((DEPTH, 6)),
            dma((DEPTH, 6)),
            dma((DEPTH, 6)),
            dma((DEPTH, PER)),
            dma((DEPTH, PER)),
            dma((DEPTH + 1,)),
            dma((DEPTH + 1,)),
            dma((3,)),
            dma((3,)),
        ],
        compiler_params=pltpu.CompilerParams(
            collective_id=1, has_side_effects=True, vmem_limit_bytes=60 << 20
        ),
    )(normed, routes, hidden, w_gate, w_up, w_down)


def per_device(
    attn_heads, out_proj, residual, norm_gain, route_ids, route_weights, w_gate, w_up, w_down
):
    hidden, normed, routes = attention(
        attn_heads, out_proj.T, residual, norm_gain, route_ids.T, route_weights.T
    )
    layer_out = experts(normed, routes, hidden, w_gate[0], w_up[0], w_down[0])
    return layer_out.astype(jnp.bfloat16)


def solution(mesh):
    placed = (
        P("expert", "tensor"),
        P("tensor", "expert"),
        P("expert", None),
        P(),
        P("expert", None),
        P("expert", None),
        P("expert", None, "tensor"),
        P("expert", None, "tensor"),
        P("expert", "tensor", None),
    )
    return jax.shard_map(
        per_device, mesh=mesh, in_specs=placed, out_specs=P("expert", "tensor"), check_vma=False
    )
```

```python
import jax
import jax.numpy as jnp
from jax import lax
from jax.experimental import pallas as pl
from jax.experimental.pallas import tpu as pltpu
from jax.sharding import PartitionSpec as P

MESH = pl.DeviceIdType.MESH
EXPERTS = 64
RING = 16
ROWS_Y = EXPERTS // RING
MAIN = 16
OVER = 2
LANES = 128
GROUPS = 8
SPLIT = 768
DEPTH = 8
PER = 8
CHUNK_MAIN = PER * MAIN
CHUNK_OVER = PER * OVER
CHUNK_ROWS = CHUNK_MAIN + CHUNK_OVER
HALF_IN = CHUNK_MAIN // 2
HALF_OUT = CHUNK_ROWS // 2 // 16 * 16


def attention_kernel(
    heads_hbm, proj_hbm, residual_hbm, gain_hbm, route_ids, route_weights,
    hidden_out, normed_out, routes_out,
    shard, sibling_shard, weight, heads, to_far, to_right, to_left, own,
    far_a, far_b, from_left, from_right, mine, arrived, residual, gain, squares,
    shared, shared_residual, shared_gain,
    local_sem, shard_sem, zsend, zrecv, csend, crecv, hsend, hrecv, rsend, rrecv, wsend, wrecv, nsend, nrecv,
    ssend, srecv,
):
    me = lax.axis_index("expert")
    x = lax.axis_index("tensor")
    y, zc = lax.div(me, RING), lax.rem(me, RING)
    core, z = lax.rem(zc, 2), lax.div(zc, 2)
    depth = RING // 2
    right, left, far = lax.rem(x + 1, 4), lax.rem(x + 3, 4), lax.rem(x + 2, 4)
    sibling = me + 1 - 2 * core
    cols = from_left.shape[1]
    half = weight.shape[1] // 2
    tokens = heads.shape[1]

    def along_z(step):
        return y * RING + lax.rem(z + depth + step, depth) * 2 + core

    def along_y(step):
        return lax.rem(y + step, ROWS_Y) * RING + zc

    partner = (x * RING + zc, y)
    local = [
        pltpu.make_async_copy(proj_hbm, shard, local_sem.at[0]),
        pltpu.make_async_copy(heads_hbm, heads.at[y], local_sem.at[1]),
        pltpu.make_async_copy(
            residual_hbm.at[:, pl.ds(pl.multiple_of(x * cols, cols), cols)], residual, local_sem.at[2]
        ),
        pltpu.make_async_copy(
            gain_hbm.at[:, pl.ds(pl.multiple_of(x * cols, cols), cols)], gain, local_sem.at[3]
        ),
    ]
    share = cols - SPLIT
    for m in range(4):
        local.append(
            pltpu.make_async_copy(
                residual_hbm.at[:, pl.ds(m * cols + SPLIT, share)],
                shared_residual.at[:, pl.ds(m * share, share)],
                local_sem.at[4 + m],
            )
        )
        local.append(
            pltpu.make_async_copy(
                gain_hbm.at[:, pl.ds(m * cols + SPLIT, share)],
                shared_gain.at[:, pl.ds(m * share, share)],
                local_sem.at[8 + m],
            )
        )
    for copy in local:
        copy.start()

    barrier = pltpu.get_barrier_semaphore()
    for device in (sibling, along_z(1), along_z(-1), along_y(1), along_y(2), along_y(3)):
        pl.semaphore_signal(barrier, inc=1, device_id=(device, x), device_id_type=MESH)
    for m in (right, left, far):
        pl.semaphore_signal(barrier, inc=1, device_id=(me, m), device_id_type=MESH)

    @pl.when(x != y)
    def _():
        pl.semaphore_signal(barrier, inc=1, device_id=partner, device_id_type=MESH)
        pl.semaphore_wait(barrier, 10)

    @pl.when(x == y)
    def _():
        pl.semaphore_wait(barrier, 9)

    def remote(source, landing, send, recv, device):
        return pltpu.make_async_remote_copy(
            src_ref=source,
            dst_ref=landing,
            send_sem=send,
            recv_sem=recv,
            device_id=device,
            device_id_type=MESH,
        )

    swap_shard = remote(
        shard.at[:, pl.ds(pl.multiple_of((1 - core) * half, half), half)],
        sibling_shard,
        shard_sem.at[0],
        shard_sem.at[1],
        (sibling, x),
    )
    local[0].wait()
    swap_shard.start()
    local[1].wait()

    def share_heads(i):
        return remote(heads.at[y], heads.at[y], hsend.at[i], hrecv.at[i], (along_y(i + 1), x))

    for i in (1, 0, 2):
        share_heads(i).start()

    def piece(owner, part):
        start = core * half + (half // 2 if part == 2 else 0)
        count = half if part == 0 else half // 2
        return weight.at[owner, pl.ds(pl.multiple_of(start, half // 2), count)]

    def ring(direction, s):
        offset = -(s - 1) if direction == 0 else s - 1
        ref = piece(
            lax.rem(z + depth + offset, depth), (1 + direction) if s == depth // 2 else 0
        )
        target = along_z(1 if direction == 0 else -1)
        return remote(ref, ref, zsend.at[direction, s - 1], zrecv.at[direction, s - 1], (target, x))

    def across(direction, s):
        offset = -s if direction == 0 else s
        ref = piece(
            lax.rem(z + depth + offset, depth), (1 + direction) if s == depth // 2 else 0
        )
        i = 5 * direction + s
        return remote(ref, ref, csend.at[i], crecv.at[i], (sibling, x))

    width = shard.shape[0]
    row = lax.broadcasted_iota(jnp.int32, (LANES, width), 0)
    lane = lax.broadcasted_iota(jnp.int32, (LANES, width), 1)
    put_own = (row == lane + width * core).astype(jnp.bfloat16)
    put_other = (row == lane + width * (1 - core)).astype(jnp.bfloat16)
    swap_shard.wait_recv()
    both = jnp.dot(
        put_own,
        shard[:, pl.ds(pl.multiple_of(core * half, half), half)],
        preferred_element_type=jnp.float32,
    ) + jnp.dot(put_other, sibling_shard[...], preferred_element_type=jnp.float32)
    both = both.T
    weight[z, pl.ds(pl.multiple_of(core * half, half), half)] = both.astype(jnp.bfloat16)
    ring(0, 1).start()
    ring(1, 1).start()
    across(0, 0).start()
    square = (tokens, LANES)
    row = lax.broadcasted_iota(jnp.int32, square, 0)
    earlier = jnp.where(row < lax.broadcasted_iota(jnp.int32, square, 1), 1.0, 0.0)
    ids = route_ids[...]
    ahead_z = (((ids & (RING - 1)) >> 1) + depth - z) & (depth - 1)
    chunk = jnp.where(
        ahead_z == 0, 0, jnp.where(ahead_z <= depth // 2, 2 * ahead_z - 1, 2 * (depth - ahead_z))
    )
    ahead_y = ((ids >> 4) + ROWS_Y - y) & (ROWS_Y - 1)
    relative = chunk * PER + ahead_y * 2 + ((ids + 2 - core) & 1)
    shares = route_weights[...] / jnp.sum(route_weights[...], axis=0, keepdims=True)
    chosen = jnp.zeros(square, jnp.float32)
    scaled = jnp.zeros(square, jnp.float32)
    for k in range(ids.shape[0]):
        hit = row == relative[k : k + 1]
        chosen = jnp.where(hit, 1.0, chosen)
        scaled = jnp.where(hit, shares[k : k + 1], scaled)
    rank = jnp.dot(
        chosen.astype(jnp.bfloat16),
        earlier.astype(jnp.bfloat16),
        preferred_element_type=jnp.float32,
    )
    rank = jnp.where(chosen > 0, rank, -1.0)
    for i in range(depth):
        routes_out[i, :PER] = rank[i * PER : (i + 1) * PER]
        routes_out[i, PER:] = scaled[i * PER : (i + 1) * PER]

    for s in range(1, depth // 2 + 1):
        for direction in (0, 1):
            ring(direction, s).wait_recv()
            if s < depth // 2:
                ring(direction, s + 1).start()
            across(direction, s).start()
    handed = [(0, 0)] + [(d, s) for s in range(1, depth // 2 + 1) for d in (0, 1)]
    for i in (0, 2, 1):
        share_heads(i).wait_recv()
    for d, s in handed:
        across(d, s).wait_recv()

    def partial(block):
        return jnp.concatenate(
            [
                jnp.dot(
                    heads[block],
                    jnp.concatenate([weight[i], weight[i + 1]], axis=1),
                    preferred_element_type=jnp.float32,
                )
                for i in range(0, RING // 2, 2)
            ],
            axis=1,
        )

    part = tokens // 2

    def reduce(i):
        rows = pl.ds((0, part, part, 0, 0, part)[i], part)
        source = (to_far, to_far, to_right, to_left, to_right, to_left)[i].at[rows]
        landing = (
            far_a,
            far_b,
            from_left.at[rows],
            from_right.at[rows],
            from_left.at[rows],
            from_right.at[rows],
        )[i]
        target = (right, left)[i % 2]
        return remote(source, landing, rsend.at[i], rrecv.at[i], (me, target))

    def exchange(i):
        rows = pl.ds(i * part, part)
        return remote(mine.at[rows], arrived.at[rows], wsend.at[i], wrecv.at[i], partner)

    to_far[...] = partial(far).astype(jnp.bfloat16)
    reduce(0).start()
    reduce(1).start()
    via_right = partial(right)
    to_right[part:] = via_right[part:].astype(jnp.bfloat16)
    reduce(2).start()
    via_left = partial(left)
    to_left[:part] = via_left[:part].astype(jnp.bfloat16)
    reduce(3).start()
    reduce(0).wait_recv()
    to_right[:part] = (via_right[:part] + far_a[...].astype(jnp.float32)).astype(jnp.bfloat16)
    reduce(4).start()
    reduce(1).wait_recv()
    to_left[part:] = (via_left[part:] + far_b[...].astype(jnp.float32)).astype(jnp.bfloat16)
    reduce(5).start()
    own[...] = partial(x)
    for i in range(2):
        rows = slice(i * part, (i + 1) * part)
        reduce((4, 2)[i]).wait_recv()
        reduce((3, 5)[i]).wait_recv()
        mine[rows] = (
            own[rows]
            + from_left[rows].astype(jnp.float32)
            + from_right[rows].astype(jnp.float32)
        ).astype(jnp.bfloat16)

        @pl.when(x != y)
        def _():
            exchange(i).start()

    @pl.when(x != y)
    def _():
        exchange(0).wait_recv()
        exchange(1).wait_recv()

    @pl.when(x == y)
    def _():
        arrived[...] = mine[...]

    shared[x] = arrived[:, SPLIT:]

    def share_features(i):
        return remote(
            shared.at[x], shared.at[x], ssend.at[i], srecv.at[i], (me, (right, far, left)[i])
        )

    for i in range(3):
        share_features(i).start()
    for copy in local[2:]:
        copy.wait()
    hidden = residual[...].astype(jnp.float32) + arrived[...].astype(jnp.float32)
    hidden_out[...] = hidden
    squares[0] = jnp.broadcast_to(
        jnp.sum(hidden * hidden, axis=-1, keepdims=True), square
    ).T[:PER]

    def share_squares(i):
        return remote(
            squares.at[0], squares.at[i + 1], nsend.at[i], nrecv.at[i], (me, (right, far, left)[i])
        )

    for i in range(3):
        share_squares(i).start()
    for i in range(3):
        share_squares(i).wait_recv()
        share_features(i).wait_recv()
    mean = (squares[0] + squares[1] + squares[2] + squares[3]) / (4 * cols)
    scale = jnp.broadcast_to(lax.rsqrt(mean + 1e-06)[:1], square).T[:, :1]
    normed_out[:, :SPLIT] = (hidden[:, :SPLIT] * scale * gain[:, :SPLIT]).astype(jnp.bfloat16)
    for m in range(4):
        lanes = slice(m * share, (m + 1) * share)
        value = shared_residual[:, lanes].astype(jnp.float32) + shared[m].astype(jnp.float32)
        normed_out[:, SPLIT + m * share : SPLIT + (m + 1) * share] = (
            value * scale * shared_gain[:, lanes]
        ).astype(jnp.bfloat16)

    @pl.when(x != y)
    def _():
        exchange(0).wait_send()
        exchange(1).wait_send()

    swap_shard.wait_send()
    for i in range(3):
        share_heads(i).wait_send()
        share_squares(i).wait_send()
        share_features(i).wait_send()
    for d, s in handed:
        across(d, s).wait_send()
    for s in range(1, depth // 2 + 1):
        for direction in (0, 1):
            ring(direction, s).wait_send()
    for i in range(6):
        reduce(i).wait_send()


def attention(attn_heads, out_proj, residual, norm_gain, route_ids, route_weights):
    tokens, depth = attn_heads.shape
    cols = residual.shape[1] // 4
    bf16, f32 = jnp.bfloat16, jnp.float32
    dma = pltpu.SemaphoreType.DMA
    anywhere = pl.BlockSpec(memory_space=pl.ANY)
    onchip = pl.BlockSpec(memory_space=pltpu.VMEM)
    block = pltpu.VMEM((tokens, cols), bf16)
    return pl.pallas_call(
        attention_kernel,
        out_shape=(
            jax.ShapeDtypeStruct((tokens, cols), f32),
            jax.ShapeDtypeStruct((tokens, SPLIT + 4 * (cols - SPLIT)), bf16),
            jax.ShapeDtypeStruct((DEPTH, 2 * PER, tokens), f32),
        ),
        in_specs=[anywhere] * 4 + [onchip] * 2,
        out_specs=(onchip, onchip, onchip),
        scratch_shapes=[
            pltpu.VMEM(out_proj.shape, bf16),
            pltpu.VMEM((out_proj.shape[0], depth // 2), bf16),
            pltpu.VMEM((RING // 2, depth, LANES), bf16),
            pltpu.VMEM((ROWS_Y, tokens, depth), bf16),
            block,
            block,
            block,
            pltpu.VMEM((tokens, cols), f32),
            pltpu.VMEM((tokens // 2, cols), bf16),
            pltpu.VMEM((tokens // 2, cols), bf16),
            block,
            block,
            block,
            block,
            block,
            pltpu.VMEM((1, cols), f32),
            pltpu.VMEM((4, PER, LANES), f32),
            pltpu.VMEM((4, tokens, cols - SPLIT), bf16),
            pltpu.VMEM((tokens, 4 * (cols - SPLIT)), bf16),
            pltpu.VMEM((1, 4 * (cols - SPLIT)), f32),
            dma((12,)),
            dma((2,)),
            dma((2, 4)),
            dma((2, 4)),
            dma((10,)),
            dma((10,)),
            dma((3,)),
            dma((3,)),
            dma((6,)),
            dma((6,)),
            dma((2,)),
            dma((2,)),
            dma((3,)),
            dma((3,)),
            dma((3,)),
            dma((3,)),
        ],
        compiler_params=pltpu.CompilerParams(
            collective_id=2, has_side_effects=True, vmem_limit_bytes=60 << 20
        ),
    )(attn_heads, out_proj, residual, norm_gain[None, :], route_ids, route_weights)


def expert_kernel(
    normed, routes_in, hidden, gate_hbm, up_hbm, down_hbm, out,
    tokens_in, routes, packed, inbox, inner, gate_up, down, acc,
    to_far, to_right, to_left, own, far_a, far_b, from_left, from_right,
    returned, planes, total, summed, staged, quarters,
    local_sem, zsend, zrecv, tsend, trecv, ysend, yrecv, asend, arecv,
    rsend, rrecv, bsend, brecv, msend, mrecv, fsend, frecv,
):
    me = lax.axis_index("expert")
    x = lax.axis_index("tensor")
    y, zc = lax.div(me, RING), lax.rem(me, RING)
    core, z = lax.rem(zc, 2), lax.div(zc, 2)
    right, left, far = lax.rem(x + 1, 4), lax.rem(x + 3, 4), lax.rem(x + 2, 4)
    ff = gate_hbm.shape[1]
    cols = hidden.shape[1]
    share = cols - SPLIT
    inner_width = SPLIT + LANES
    first = inner_width
    last = first + 4 * share
    bf16, f32 = jnp.bfloat16, jnp.float32

    def along_z(step):
        return y * RING + lax.rem(z + DEPTH + step, DEPTH) * 2 + core

    def distance(i):
        odd = lax.rem(i, 2)
        return lax.rem(odd * lax.div(i + 1, 2) + (1 - odd) * (DEPTH - lax.div(i, 2)), DEPTH)

    def plane(dy, dc):
        return lax.rem(y + ROWS_Y + dy, ROWS_Y) * RING + z * 2 + lax.rem(core + dc, 2)

    def remote(source, landing, send, recv, device):
        return pltpu.make_async_remote_copy(
            src_ref=source,
            dst_ref=landing,
            send_sem=send,
            recv_sem=recv,
            device_id=device,
            device_id_type=MESH,
        )

    weights = [
        pltpu.make_async_copy(gate_hbm, gate_up.at[:, pl.ds(0, ff)], local_sem.at[0]),
        pltpu.make_async_copy(up_hbm, gate_up.at[:, pl.ds(ff, ff)], local_sem.at[1]),
        pltpu.make_async_copy(down_hbm, down, local_sem.at[2]),
    ]
    load_tokens = pltpu.make_async_copy(normed, tokens_in.at[0], local_sem.at[3])
    load_routes = pltpu.make_async_copy(routes_in.at[0], routes.at[0], local_sem.at[4])
    load_tokens.start()
    load_routes.start()
    for copy in weights:
        copy.start()

    barrier = pltpu.get_barrier_semaphore()

    @pl.loop(1, DEPTH)
    def _(i):
        pl.semaphore_signal(barrier, inc=1, device_id=(along_z(i), x), device_id_type=MESH)
        pl.semaphore_signal(
            barrier,
            inc=1,
            device_id=(plane(lax.div(i, 2), lax.rem(i, 2)), x),
            device_id_type=MESH,
        )

    for m in (right, far, left):
        pl.semaphore_signal(barrier, inc=1, device_id=(me, m), device_id_type=MESH)
    pl.semaphore_wait(barrier, 2 * (DEPTH - 1) + 3)

    def block(k):
        return pl.ds(pl.multiple_of(k * MAIN, MAIN), MAIN)

    def send_routes(i):
        return remote(
            routes_in.at[i], routes.at[i], tsend.at[i], trecv.at[i], (along_z(distance(i)), x)
        )

    def ring(i, before=None):
        before = lax.rem(i + DEPTH - 2, DEPTH) if before is None else before
        return remote(
            tokens_in.at[before],
            tokens_in.at[i],
            zsend.at[i],
            zrecv.at[i],
            (along_z(2 * lax.rem(i, 2) - 1), x),
        )

    middle = tokens_in.shape[1] // 2

    def ring_far(side):
        rows = pl.ds(side * middle, middle)
        return remote(
            tokens_in.at[DEPTH - 3 + side, rows],
            tokens_in.at[DEPTH - 1, rows],
            zsend.at[DEPTH - 1 + side],
            zrecv.at[DEPTH - 1 + side],
            (along_z(1 - 2 * side), x),
        )

    load_tokens.wait()
    ring(1, 0).start()
    ring(2, 0).start()

    @pl.loop(1, DEPTH)
    def _(i):
        send_routes(i).start()

    load_routes.wait()

    def exchange(i, k):
        return remote(
            packed.at[i, block(k)],
            inbox.at[i, block(k)],
            ysend.at[i, k],
            yrecv.at[i, k],
            (plane(lax.div(k, 2), lax.rem(k, 2)), x),
        )

    def give_back(i, k):
        return remote(
            packed.at[i, block(k)],
            returned.at[i, block(k)],
            bsend.at[i, k],
            brecv.at[i, k],
            (plane(-lax.div(k, 2), lax.rem(k, 2)), x),
        )

    low, high = pl.ds(0, HALF_IN), pl.ds(HALF_IN, HALF_IN)

    def gather(c, i):
        owner = (x, x, x, x, left, right)[i]
        part = (low, high, high, low, low, high)[i]
        target = (right, right, left, left, right, left)[i]
        ref = inner.at[c, owner, part]
        return remote(ref, ref, asend.at[c, i], arecv.at[c, i], (me, target))

    head, tail = pl.ds(0, HALF_OUT), pl.ds(HALF_OUT, CHUNK_ROWS - HALF_OUT)

    def reduce(c, i):
        rows = (head, tail, tail, head, head, tail)[i]
        source = (to_far, to_far, to_right, to_left, to_right, to_left)[i].at[c, rows]
        landing = (
            far_a.at[c],
            far_b.at[c],
            from_left.at[c, rows],
            from_right.at[c, rows],
            from_left.at[c, rows],
            from_right.at[c, rows],
        )[i]
        target = (right, left)[i % 2]
        return remote(source, landing, rsend.at[c, i], rrecv.at[c, i], (me, target))

    half_tokens = tokens_in.shape[1] // 2

    def send_plane(i):
        slot = (0, 1, 2, 3, 0, 7, 4, 5, 6)[i]
        step = (0, -1, 1, -2, 2, -3, 1, -1, 1)[i]
        source, landing = tokens_in.at[min(i, 7)], planes.at[slot]
        if i >= 7:
            rows = pl.ds((i - 7) * half_tokens, half_tokens)
            source, landing = tokens_in.at[7, rows], planes.at[slot, rows]
        return remote(source, landing, msend.at[i], mrecv.at[i], (along_z(step), x))

    def send_quarter(i):
        m = (right, far, left)[i]
        return remote(
            staged.at[:, pl.ds(pl.multiple_of(m * share, share), share)],
            quarters.at[i],
            fsend.at[i],
            frecv.at[i],
            (me, m),
        )

    square = (CHUNK_MAIN, CHUNK_MAIN)
    row = lax.broadcasted_iota(jnp.int32, square, 0)
    row_slot = (row & (MAIN - 1)).astype(f32)
    row_over = (MAIN + ((row & (MAIN - 1)) >> 3)).astype(f32)
    row_group = row & (GROUPS - 1)
    lane_group = lax.broadcasted_iota(jnp.int32, square, 1) & (GROUPS - 1)

    lane = lax.broadcasted_iota(jnp.int32, square, 1)

    def unsorted_row(r):
        return ((r >> 1) & (PER - 1)) * MAIN + (r & 1) * GROUPS + (r >> 4)

    sort = jnp.where(lane == unsorted_row(row), 1.0, 0.0).astype(bf16)
    unsort = jnp.where(row == unsorted_row(lane), 1.0, 0.0).astype(bf16)

    def spread(values):
        return jnp.broadcast_to(values[:, None, :], (PER, MAIN, LANES)).reshape(square)

    def dot(a, b):
        return jnp.dot(a, b, preferred_element_type=f32)

    def pick(i):
        rank = spread(routes[i, :PER])
        tokens = tokens_in[i]
        chosen = dot(jnp.where(rank == row_slot, 1.0, 0.0).astype(bf16), tokens)
        packed[i, :, :SPLIT] = chosen[:, :SPLIT].astype(bf16)
        packed[i, :, first:last] = chosen[:, SPLIT:].astype(bf16)
        wide = dot(jnp.where(rank == row_over, 1.0, 0.0).astype(bf16), tokens)
        for start, count, lane in ((0, SPLIT // LANES, SPLIT), (SPLIT, GROUPS, last)):
            tile = jnp.zeros(square, f32)
            for g in range(count):
                piece = wide[:, start + g * LANES : start + (g + 1) * LANES]
                tile = jnp.where(row_group == g, piece, tile)
            packed[i, :, lane : lane + LANES] = tile.astype(bf16)
        inbox[i, :MAIN] = packed[i, :MAIN]

        @pl.loop(1, PER)
        def _(k):
            exchange(i, 1 + lax.rem(k + 2, PER - 1)).start()

    def project(act, quarter):
        columns = pl.ds(pl.multiple_of(quarter * cols, cols), cols)
        return dot(act, down[:, columns])

    def compute(c):
        @pl.loop(1, PER)
        def _(k):
            exchange(c, k).wait_send()

        tails = jnp.concatenate(
            [inner[c, m, :, SPLIT:] for m in range(4)] + [inbox[c, :, last:]], axis=1
        )
        tails = dot(sort, tails).astype(bf16)

        def tail_piece(g, tile):
            return tails[g * CHUNK_OVER : (g + 1) * CHUNK_OVER, tile * LANES : (tile + 1) * LANES]

        per_share = share // LANES
        for m in range(4):
            extra = [tail_piece(g, m) for g in range(SPLIT // LANES)] + [
                tail_piece(m * per_share + g, 4) for g in range(per_share)
            ]
            body = jnp.concatenate(
                [
                    inner[c, m, :, :SPLIT],
                    inbox[c, :, first + m * share : first + (m + 1) * share],
                ],
                axis=1,
            )
            rows = jnp.concatenate([body, jnp.concatenate(extra, axis=1)], axis=0)
            part = dot(rows, gate_up[m * cols : (m + 1) * cols, :])
            if m == 0:
                acc[...] = part
            else:
                acc[...] += part
        gate, up = acc[:, :ff], acc[:, ff:]
        act = (gate / (1.0 + jnp.exp(-gate)) * up).astype(bf16)

        def keep_share(quarter, value):
            lanes = pl.ds(pl.multiple_of(first + quarter * share, LANES), share)
            packed[c, :, lanes] = value[:CHUNK_MAIN, SPLIT:].astype(bf16)
            staging = pl.ds(pl.multiple_of(quarter * share, share), share)
            staged[:CHUNK_OVER, staging] = value[CHUNK_MAIN:, SPLIT:].astype(bf16)

        value = project(act, far)
        to_far[c] = value[:, :SPLIT].astype(bf16)
        reduce(c, 0).start()
        reduce(c, 1).start()
        keep_share(far, value)
        value = project(act, right)
        to_right[c] = value[:, :SPLIT].astype(bf16)
        reduce(c, 2).start()
        keep_share(right, value)
        value = project(act, left)
        to_left[c] = value[:, :SPLIT].astype(bf16)
        reduce(c, 3).start()
        keep_share(left, value)
        value = project(act, x)
        own[c] = value[:, :SPLIT]
        keep_share(x, value)
        over = staged[:CHUNK_OVER, :]
        over = jnp.concatenate(
            [over[:, g * LANES : (g + 1) * LANES] for g in range(GROUPS)], axis=0
        )
        packed[c, :, last:] = dot(unsort, over).astype(bf16)

    def finish(c):
        for i in (2, 3, 4, 5):
            reduce(c, i).wait_recv()
        value = (
            own[c] + from_left[c].astype(f32) + from_right[c].astype(f32)
        ).astype(bf16)
        packed[c, :, :SPLIT] = value[:CHUNK_MAIN]
        count = SPLIT // LANES
        over = jnp.concatenate(
            [value[CHUNK_MAIN:, g * LANES : (g + 1) * LANES] for g in range(count)]
            + [jnp.zeros(((GROUPS - count) * CHUNK_OVER, LANES), bf16)],
            axis=0,
        )
        packed[c, :, SPLIT:first] = dot(unsort, over).astype(bf16)
        returned[c, :MAIN] = packed[c, :MAIN]

        @pl.loop(1, PER)
        def _(k):
            give_back(c, 1 + lax.rem(k + 2, PER - 1)).start()

    def combine(c):
        @pl.loop(1, PER)
        def _(k):
            give_back(c, k).wait_recv()

        rank, weight = spread(routes[c, :PER]), spread(routes[c, PER:])
        rows = returned[c]
        whole = jnp.where(rank == row_slot, weight, 0.0).T
        over = jnp.where(rank == row_over, weight, 0.0).T
        high_part = whole.astype(bf16)
        low_part = (whole - high_part.astype(f32)).astype(bf16)
        mixed = dot(high_part, rows) + dot(low_part, rows)
        tiles = jnp.concatenate([rows[:, SPLIT:first], rows[:, last:]], axis=1)
        extra = []
        for g in range(GROUPS):
            picked = jnp.where(lane_group == g, over, 0.0)
            high_part = picked.astype(bf16)
            low_part = (picked - high_part.astype(f32)).astype(bf16)
            extra.append(dot(high_part, tiles) + dot(low_part, tiles))
        count = SPLIT // LANES
        inner_sum = mixed[:, :SPLIT] + jnp.concatenate(
            [extra[g][:, :LANES] for g in range(count)], axis=1
        )
        share_sum = mixed[:, first:last] + jnp.concatenate(
            [extra[g][:, LANES:] for g in range(GROUPS)], axis=1
        )

        @pl.when(c == 0)
        def _():
            total[:, :SPLIT] = inner_sum
            total[:, SPLIT:] = share_sum

        @pl.when((c >= 1) & (c <= DEPTH - 4))
        def _():
            ring(c + 2).wait_send()

        for side in (0, 1):

            @pl.when(c == DEPTH - 3 + side)
            def _():
                ring_far(side).wait_send()

        @pl.when(c > 0)
        def _():
            summed[:, :SPLIT] = inner_sum
            summed[:, SPLIT:] = share_sum

        for side in (0, 1):
            rows = slice(side * half_tokens, (side + 1) * half_tokens)

            @pl.when(c == 5 + side)
            def _():
                send_plane(7 + side).wait_recv()
                summed[rows] += planes[5 + side, rows].astype(f32)

        @pl.when(c == 4)
        def _():
            send_plane(6).wait_recv()
            summed[...] += planes[4].astype(f32)

        @pl.when(c > 0)
        def _():
            tokens_in[c] = summed[...].astype(bf16)

        for i in range(1, DEPTH):

            @pl.when(c == i)
            def _():
                send_plane(i).start()
                if i == 7:
                    send_plane(8).start()

    def order(p):
        late = lax.div(p + 4, DEPTH)
        return (1 - late) * p + late * (11 - p)

    pick(0)

    @pl.loop(0, DEPTH + 5)
    def _(t):
        @pl.when((t >= 1) & (t < DEPTH + 1))
        def _():
            c = order(t - 1)
            gather(c, 0).wait_recv()
            gather(c, 4).start()
            gather(c, 2).wait_recv()
            gather(c, 5).start()

        @pl.when(t < DEPTH)
        def _():
            c = order(t)

            @pl.loop(1, PER)
            def _(k):
                exchange(c, k).wait_recv()

            inner[c, x] = inbox[c, :, :inner_width]
            for i in (0, 2, 1, 3):
                gather(c, i).start()

        @pl.when((t >= DEPTH // 2) & (t + 1 < DEPTH))
        def _():
            i = order(t + 1)
            send_routes(i).wait_recv()
            pick(i)

        @pl.when(t == 2)
        def _():
            for copy in weights:
                copy.wait()

        @pl.when((t >= 2) & (t < DEPTH + 2))
        def _():
            c = order(t - 2)
            for i in (1, 3, 4, 5):
                gather(c, i).wait_recv()
            compute(c)

        @pl.when((t >= 3) & (t < DEPTH + 3))
        def _():
            c = order(t - 3)
            reduce(c, 0).wait_recv()
            to_right[c, :HALF_OUT] = (
                to_right[c, :HALF_OUT].astype(f32) + far_a[c].astype(f32)
            ).astype(bf16)
            reduce(c, 4).start()
            reduce(c, 1).wait_recv()
            to_left[c, HALF_OUT:] = (
                to_left[c, HALF_OUT:].astype(f32) + far_b[c].astype(f32)
            ).astype(bf16)
            reduce(c, 5).start()

        @pl.when((t >= 4) & (t < DEPTH + 4))
        def _():
            finish(order(t - 4))

        @pl.when(t >= 5)
        def _():
            combine(order(t - 5))

        @pl.when(t < 3)
        def _():
            for side in (0, 1):
                i = 2 * t + 1 + side
                ring(i).wait_recv()

                @pl.when(t < 2)
                def _():
                    ring(i + 2).start()

                @pl.when(t == 2)
                def _():
                    ring_far(side).start()

        @pl.when(t == 3)
        def _():
            for side in (0, 1):
                ring_far(side).wait_recv()

        @pl.when(t < DEPTH // 2)
        def _():
            i = order(t + 1)
            send_routes(i).wait_recv()
            pick(i)

    for i, slot in ((1, 1), (2, 2), (3, 3), (5, 7), (4, 0)):
        send_plane(i).wait_recv()
        total[...] += planes[slot].astype(f32)

    staged[...] = total[:, SPLIT:].astype(bf16)
    for i in range(3):
        send_quarter(i).start()
    out[:, :SPLIT] = hidden[:, :SPLIT] + total[:, :SPLIT]
    mixture = total[:, pl.ds(pl.multiple_of(SPLIT + x * share, share), share)]
    for i in range(3):
        send_quarter(i).wait_recv()
        mixture += quarters[i].astype(f32)
    out[:, SPLIT:] = hidden[:, SPLIT:] + mixture

    for i in (1, 2):
        ring(i, 0).wait_send()
    for i in range(3):
        send_quarter(i).wait_send()

    @pl.loop(1, DEPTH)
    def _(i):
        send_routes(i).wait_send()

    for i in range(1, DEPTH + 1):
        send_plane(i).wait_send()

    @pl.loop(0, DEPTH)
    def _(c):
        for i in range(6):
            gather(c, i).wait_send()
            reduce(c, i).wait_send()

        @pl.loop(1, PER)
        def _(k):
            give_back(c, k).wait_send()


def experts(normed, routes, hidden, w_gate, w_up, w_down):
    tokens, wide = normed.shape
    cols = hidden.shape[1]
    ff, model_width = w_down.shape
    rows = CHUNK_ROWS
    width = wide + 2 * LANES
    bf16, f32 = jnp.bfloat16, jnp.float32
    dma = pltpu.SemaphoreType.DMA
    anywhere = pl.BlockSpec(memory_space=pl.ANY)
    onchip = pl.BlockSpec(memory_space=pltpu.VMEM)
    moved = pltpu.VMEM((DEPTH, rows, SPLIT), bf16)
    return pl.pallas_call(
        expert_kernel,
        out_shape=jax.ShapeDtypeStruct((tokens, cols), f32),
        in_specs=[anywhere] * 2 + [onchip] + [anywhere] * 3,
        out_specs=onchip,
        scratch_shapes=[
            pltpu.VMEM((DEPTH, tokens, wide), bf16),
            pltpu.VMEM((DEPTH, 2 * PER, LANES), f32),
            pltpu.VMEM((DEPTH, CHUNK_MAIN, width), bf16),
            pltpu.VMEM((DEPTH, CHUNK_MAIN, width), bf16),
            pltpu.VMEM((DEPTH, 4, CHUNK_MAIN, SPLIT + LANES), bf16),
            pltpu.VMEM((model_width, 2 * ff), bf16),
            pltpu.VMEM((ff, model_width), bf16),
            pltpu.VMEM((rows, 2 * ff), f32),
            moved,
            moved,
            moved,
            pltpu.VMEM((DEPTH, rows, SPLIT), f32),
            pltpu.VMEM((DEPTH, HALF_OUT, SPLIT), bf16),
            pltpu.VMEM((DEPTH, rows - HALF_OUT, SPLIT), bf16),
            moved,
            moved,
            pltpu.VMEM((DEPTH, CHUNK_MAIN, width), bf16),
            pltpu.VMEM((DEPTH, tokens, wide), bf16),
            pltpu.VMEM((tokens, wide), f32),
            pltpu.VMEM((tokens, wide), f32),
            pltpu.VMEM((tokens, wide - SPLIT), bf16),
            pltpu.VMEM((3, tokens, cols - SPLIT), bf16),
            dma((5,)),
            dma((DEPTH + 1,)),
            dma((DEPTH + 1,)),
            dma((DEPTH,)),
            dma((DEPTH,)),
            dma((DEPTH, PER)),
            dma((DEPTH, PER)),
            dma((DEPTH, 6)),
            dma((DEPTH, 6)),
            dma((DEPTH, 6)),
            dma((DEPTH, 6)),
            dma((DEPTH, PER)),
            dma((DEPTH, PER)),
            dma((DEPTH + 1,)),
            dma((DEPTH + 1,)),
            dma((3,)),
            dma((3,)),
        ],
        compiler_params=pltpu.CompilerParams(
            collective_id=1, has_side_effects=True, vmem_limit_bytes=60 << 20
        ),
    )(normed, routes, hidden, w_gate, w_up, w_down)


def per_device(
    attn_heads, out_proj, residual, norm_gain, route_ids, route_weights, w_gate, w_up, w_down
):
    hidden, normed, routes = attention(
        attn_heads, out_proj.T, residual, norm_gain, route_ids.T, route_weights.T
    )
    layer_out = experts(normed, routes, hidden, w_gate[0], w_up[0], w_down[0])
    return layer_out.astype(jnp.bfloat16)


def solution(mesh):
    placed = (
        P("expert", "tensor"),
        P("tensor", "expert"),
        P("expert", None),
        P(),
        P("expert", None),
        P("expert", None),
        P("expert", None, "tensor"),
        P("expert", None, "tensor"),
        P("expert", "tensor", None),
    )
    return jax.shard_map(
        per_device, mesh=mesh, in_specs=placed, out_specs=P("expert", "tensor"), check_vma=False
    )
```
